512 devices in a mesh: row: 32 (over z, core), col: 16 (over x, y).
Axes of the slice: x: 4, y: 4, z: 16, core: 2. Of those that a mesh axis runs over, the one named last changes fastest.
Arguments:
- trailing: float32 [16384, 16384], P('row', 'col'), may hold values from -6 to 6
- panel: float32 [16384, 512], P(('row', 'col')), may hold values from -0.25 to 0.25
- inv_factor: float32 [512, 512], P(None, 'col'), as said below
- later_series: float32 [16384, 1024], P('row', 'col'), may hold values from -6 to 6
- fold_series: float32 [512, 1024], P('row', 'col'), may hold values from -6 to 6
- fold_len: int32 [1024], P('col'), may hold values from 1 to 32, as said below
Outputs:
- new_trailing: float32 [16384, 16384], P('row', 'col')
- new_series: float32 [16384, 1024], P('row', 'col')
The draws below stay inside these ranges and needn't reach their ends.
Inputs may be any that keep to these rules, and one draw needn't show every extreme that they name: inv_factor is lower triangular with a diagonal between 1 and 2. `fold_len`: some series reach all 32 blocks and some only one.
All inputs are finite; a program needn't handle non-finite values.
Results may differ from the reference program's by a relative error of at most 0.0003.
Values sent between devices are 32-bit elements; how exact they have to be, the bound alone decides.
No kernel may reach another device: no remote copies, remote signals or barrier semaphores. Data moves between devices by JAX's collectives and lax.ppermute only.
A program may use at most 64 MiB of HBM per device.

```python
import math
import jax
import jax.numpy as jnp
from jax import lax

PANEL = 512
SERIES = 1024
ORDER = 16384
BLOCKS = 32


def draw_inv_factor(key, part):
    inner = jax.random.fold_in(key, 7)
    first, second = jax.random.split(inner)
    diag_part = jax.random.uniform(first, (PANEL,), jnp.float32, 1.0, 2.0)
    spread = 0.6 / math.sqrt(PANEL)
    lower = jnp.tril(jax.random.normal(second, (PANEL, PANEL), jnp.float32) * spread, -1)
    return lower + jnp.diag(diag_part)


def draw_fold_len(key, part):
    inner = jax.random.fold_in(key, 11)
    values = jax.random.randint(inner, (SERIES,), 1, BLOCKS + 1, dtype=jnp.int32)
    return values.at[0].set(BLOCKS).at[1].set(1)


def block_levels(stream_key, shape, pieces, low, top_value):
    factor_of = 1.0
    for position, shards_of in pieces:
        draws = jax.random.uniform(jax.random.fold_in(jax.random.fold_in(stream_key, 6), position), (shards_of,), jnp.float32, low / len(pieces), top_value / len(pieces))
        factor_of = factor_of * jnp.repeat(jnp.exp(draws), shape[position] // shards_of).reshape((-1,) + (1,) * (len(shape) - 1 - position))
    return factor_of


def noise(rng, shape, width, most, cuts=(), kind=jnp.bfloat16):
    values = width * jax.random.normal(rng, shape, jnp.float32)
    if cuts:
        values = values * block_levels(rng, shape, cuts, -0.22, 0.18)
    return jnp.clip(values, -most, most).astype(kind)


def setup_inputs(seed: int = 0) -> dict:
    keys = jax.random.split(jax.random.key(seed), 7)
    return {
        "trailing": noise(keys[0], (ORDER, ORDER), 1.0, 6.0, ((0, 32), (1, 16)), jnp.float32),
        "panel": noise(keys[1], (ORDER, PANEL), PANEL ** -0.5, 0.25, ((0, 512),), jnp.float32),
        "inv_factor": draw_inv_factor(jax.random.fold_in(keys[6], 71), 0),
        "later_series": noise(keys[3], (ORDER, SERIES), 1.0, 6.0, ((0, 32), (1, 16)), jnp.float32),
        "fold_series": noise(keys[4], (PANEL, SERIES), 1.0, 6.0, ((0, 32), (1, 16)), jnp.float32),
        "fold_len": draw_fold_len(jax.random.fold_in(keys[6], 71), 0),
    }


def reference(trailing, panel, inv_factor, later_series, fold_series, fold_len):
    highest = lax.Precision.HIGHEST
    solved = jnp.dot(panel, inv_factor.T, precision=highest, preferred_element_type=jnp.float32)
    order = trailing.shape[0]
    blocks = order // PANEL
    column_tile = jnp.arange(order, dtype=jnp.int32) // PANEL

    def one_block(item):
        rows, solved_rows, index = item
        update = jnp.dot(solved_rows, solved.T, precision=highest, preferred_element_type=jnp.float32)
        return jnp.where(column_tile[None, :] <= index, rows - update, rows)

    new_trailing = lax.map(one_block, (trailing.reshape(blocks, PANEL, order), solved.reshape(blocks, PANEL, PANEL), jnp.arange(blocks, dtype=jnp.int32))).reshape(order, order)
    innovations = jnp.dot(inv_factor, fold_series, precision=highest, preferred_element_type=jnp.float32)
    correction = jnp.dot(solved, innovations, precision=highest, preferred_element_type=jnp.float32)
    row_tile = jnp.arange(order, dtype=jnp.int32) // PANEL
    active = row_tile[:, None] < fold_len[None, :]
    new_series = jnp.where(active, later_series - correction, later_series)
    return new_trailing, new_series
```

```python
import jax
import jax.numpy as jnp
from jax import lax
from jax.experimental import pallas as pl
from jax.experimental.pallas import tpu as pltpu
from jax.sharding import PartitionSpec as P


AXES = ("row", "col")
X, Y, Z, CORES = 4, 4, 16, 2
NT = (((1,), (1,)), ((), ()))
NN = (((1,), (0,)), ((), ()))


def device(x, y, z, k):
    return ((z % Z) * CORES + k) * (X * Y) + (x % X) * Y + y % Y


def pairs(move):
    out = []
    for x in range(X):
        for y in range(Y):
            for z in range(Z):
                for k in range(CORES):
                    out.append((device(x, y, z, k), device(*move(x, y, z, k))))
    return out


TRANSPOSE = pairs(lambda x, y, z, k: (z // Y, z % Y, x * Y + y, k))
SWAP = pairs(lambda x, y, z, k: (x, y, z, 1 - k))
PM2 = pairs(lambda x, y, z, k: (x, y, z + 2 if k == 0 else z - 2, k))


def shift(d):
    return pairs(lambda x, y, z, k: (x, y, z + d, k))


def send(array, moves):
    return lax.ppermute(array, AXES, moves)


def split(x):
    high = x.astype(jnp.bfloat16)
    return high, (x - high.astype(jnp.float32)).astype(jnp.bfloat16)


def dot3(a, b, dims):
    ah, al = a
    bh, bl = b
    dot = lambda u, v: lax.dot_general(u, v, dims, preferred_element_type=jnp.float32)
    return dot(ah, bh) + (dot(ah, bl) + dot(al, bh))


def pack_body(chunk, fold, out):
    for j in range(4):
        out[32 * j:32 * j + 32, :] = chunk[:, 128 * j:128 * j + 128]
    out[128:136, 0:64] = fold[0:8, :]
    out[128:136, 64:128] = fold[8:16, :]


def weight_body(gathered, other, out, rows, inv):
    k = lax.axis_index("row") % 2
    for c in range(16):
        rows[32 * c:32 * c + 32, :] = gathered[c, 0:32, :]
        inv[pl.ds(pl.multiple_of(32 * c + 16 * k, 16), 16), :] = gathered[c, 32:48, :]
        inv[pl.ds(pl.multiple_of(32 * c + 16 - 16 * k, 16), 16), :] = other[c]
    inverse = split(inv[...])
    solved = dot3(split(rows[...]), inverse, NN)
    out[...] = dot3(split(solved), inverse, NT)


OFFSETS = (0, -4, 4, 8)


def final_body(weight, mine0, mine1, mine2, mine3, theirs, trailing, series, length, out_t, out_s, cols, fold):
    row = lax.axis_index("row")
    col = lax.axis_index("col")
    z, k = row // 2, row % 2

    def place(ref, base, group, core):
        for slot in range(4):
            step = OFFSETS[slot]
            if group < 3:
                far = (0, -1, 1)[group] + step
            else:
                far = step - 2 + 4 * core
            at = (z + far + 32) % 16
            start = base + 136 * slot
            for j in range(4):
                cols[core, pl.ds(pl.multiple_of(32 * at, 32), 32), 128 * j:128 * j + 128] = ref[start + 32 * j:start + 32 * j + 32, :]
            tile = ref[start + 128:start + 136, :]
            first = pl.multiple_of(16 * (2 * at + core), 16)
            fold[pl.ds(first, 8), :] = tile[:, 0:64]
            fold[pl.ds(first + 8, 8), :] = tile[:, 64:128]

    for group, ref in enumerate((mine0, mine1, mine2, mine3)):
        place(ref, 0, group, k)
    for group in range(4):
        place(theirs, 544 * group, group, 1 - k)
    w = split(weight[...])
    for h in range(2):
        lower = 2 * col + h <= row
        span = slice(512 * h, 512 * h + 512)

        @pl.when(lower)
        def _():
            out_t[:, span] = trailing[:, span] - dot3(w, split(cols[h]), NT)

        @pl.when(jnp.logical_not(lower))
        def _():
            out_t[:, span] = trailing[:, span]

    correction = dot3(w, split(fold[...]), NN)
    active = row < length[...]
    out_s[...] = jnp.where(active, series[...] - correction, series[...])


def on_device(trailing, panel, inv_factor, later_series, fold_series, fold_len):
    f32 = jnp.float32
    k = lax.axis_index("row") % 2
    chunk = send(panel, TRANSPOSE)
    half = lax.dynamic_slice(inv_factor.T, (16 * k, 0), (16, 512))
    load = jnp.concatenate([panel, half], 0)
    gathered = lax.all_to_all(jnp.broadcast_to(load[None], (16, 48, 512)), "col", 0, 0, tiled=True)
    other = send(gathered[:, 32:, :], SWAP)
    packed = pl.pallas_call(pack_body, out_shape=jax.ShapeDtypeStruct((136, 128), f32), name="pack")(chunk, fold_series)
    far = [packed] + [send(packed, shift(d)) for d in (4, -4, 8)]
    near = jnp.concatenate(far, 0)
    mine = [near, send(near, shift(1)), send(near, shift(-1)), send(near, PM2)]
    weight = pl.pallas_call(
        weight_body,
        out_shape=jax.ShapeDtypeStruct((512, 512), f32),
        scratch_shapes=[pltpu.VMEM((512, 512), f32), pltpu.VMEM((512, 512), f32)],
        name="weight",
    )(gathered, other)
    theirs = send(jnp.concatenate(mine, 0), SWAP)
    return pl.pallas_call(
        final_body,
        out_shape=(jax.ShapeDtypeStruct((512, 1024), f32), jax.ShapeDtypeStruct((512, 64), f32)),
        scratch_shapes=[pltpu.VMEM((2, 512, 512), f32), pltpu.VMEM((512, 64), f32)],
        name="final",
    )(weight, *mine, theirs, trailing, later_series, fold_len[None, :])


def solution(mesh):
    in_specs = (
        P("row", "col"),
        P(("row", "col"), None),
        P(None, "col"),
        P("row", "col"),
        P("row", "col"),
        P("col"),
    )
    out_specs = (P("row", "col"), P("row", "col"))
    return jax.shard_map(
        on_device, mesh=mesh, in_specs=in_specs, out_specs=out_specs, check_vma=False
    )
```

```python
import jax
import jax.numpy as jnp
from jax import lax
from jax.experimental import pallas as pl
from jax.experimental.pallas import tpu as pltpu
from jax.sharding import PartitionSpec as P


AXES = ("row", "col")
X, Y, Z, CORES = 4, 4, 16, 2
NT = (((1,), (1,)), ((), ()))
NN = (((1,), (0,)), ((), ()))


def device(x, y, z, k):
    return ((z % Z) * CORES + k) * (X * Y) + (x % X) * Y + y % Y


def pairs(move):
    out = []
    for x in range(X):
        for y in range(Y):
            for z in range(Z):
                for k in range(CORES):
                    out.append((device(x, y, z, k), device(*move(x, y, z, k))))
    return out


STEPS = {
    8: (0, 0),
    7: (1, 0), 9: (3, 0), 6: (0, 1), 10: (0, 3),
    5: (1, 1), 11: (1, 3), 4: (3, 1), 12: (3, 3), 3: (2, 0), 13: (0, 2),
    2: (2, 1), 14: (2, 3), 1: (1, 2), 15: (3, 2),
    0: (2, 2),
}
PLACES = {place: step for step, place in STEPS.items()}


def table(axis):
    bits = sum(STEPS[step][axis] << (2 * step) for step in range(Z))
    return bits - (1 << 32) if bits >> 31 else bits


TABLE_X, TABLE_Y = table(0), table(1)


def transpose_move(x, y, z, k):
    cx, cy = z // Y, z % Y
    return cx, cy, z + PLACES[(x - cx) % X, (y - cy) % Y], k


TRANSPOSE = pairs(transpose_move)
SWAP = pairs(lambda x, y, z, k: (x, y, z, 1 - k))
PM2 = pairs(lambda x, y, z, k: (x, y, z + 2 if k == 0 else z - 2, k))


def shift(d):
    return pairs(lambda x, y, z, k: (x, y, z + d, k))


def send(array, moves):
    return lax.ppermute(array, AXES, moves)


def near_memory(array):
    return pltpu.with_memory_space_constraint(array, pltpu.VMEM)


def split(x):
    high = x.astype(jnp.bfloat16)
    return high, (x - high.astype(jnp.float32)).astype(jnp.bfloat16)


def dot3(a, b, dims):
    ah, al = a
    bh, bl = b
    dot = lambda u, v: lax.dot_general(u, v, dims, preferred_element_type=jnp.float32)
    return dot(ah, bh) + (dot(ah, bl) + dot(al, bh))


def pack_body(chunk, fold, out):
    for j in range(4):
        out[32 * j:32 * j + 32, :] = chunk[:, 128 * j:128 * j + 128]
    out[128:136, 0:64] = fold[0:8, :]
    out[128:136, 64:128] = fold[8:16, :]


def weight_body(gathered, other, out, rows, inv):
    k = lax.axis_index("row") % 2
    for c in range(16):
        rows[32 * c:32 * c + 32, :] = gathered[c, 0:32, :]
        inv[pl.ds(pl.multiple_of(32 * c + 16 * k, 16), 16), :] = gathered[c, 32:48, :]
        inv[pl.ds(pl.multiple_of(32 * c + 16 - 16 * k, 16), 16), :] = other[c]
    inverse = split(inv[...])
    solved = dot3(split(rows[...]), inverse, NN)
    out[...] = dot3(split(solved), inverse, NT)


OFFSETS = (0, -4, 4, 8)


def where_am_i():
    row = lax.axis_index("row")
    return row, lax.axis_index("col"), row // 2, row % 2


def place(ref, base, group, core, z, col, cols, fold):
    for slot in range(4):
        step = OFFSETS[slot]
        far = (0, -1, 1)[group] + step if group < 3 else step - 2 + 4 * core
        at = (z + far + 32) & 15
        hop = 2 * ((at - col) & 15)
        px = (col // 4 + (jnp.int32(TABLE_X) >> hop)) & 3
        py = (col + (jnp.int32(TABLE_Y) >> hop)) & 3
        rows = pl.ds(pl.multiple_of(32 * (4 * px + py), 32), 32)
        start = base + 136 * slot
        for j in range(4):
            cols[rows, 128 * j:128 * j + 128] = ref[start + 32 * j:start + 32 * j + 32, :]
        tile = ref[start + 128:start + 136, :]
        first = pl.multiple_of(16 * (2 * at + core), 16)
        fold[pl.ds(first, 8), :] = tile
        fold[pl.ds(first + 8, 8), :] = pltpu.roll(tile, 64, 1)


def join_body(a, b, c, weight, out):
    out[0:544, :] = a[...]
    out[544:1088, :] = b[...]
    out[1088:1632, :] = c[...]


def update(half, w, cols, trailing, out, vin, vout, sem_in, sem_out, row, col):
    span = pl.ds(pl.multiple_of(512 * half, 512), 512)
    lower = 2 * col + half <= row
    pltpu.make_async_copy(trailing.at[:, span], vin, sem_in).wait()

    @pl.when(lower)
    def _():
        vout[...] = vin[...] - dot3(w, split(cols[...]), NT)

    @pl.when(jnp.logical_not(lower))
    def _():
        vout[...] = vin[...]

    copy = pltpu.make_async_copy(vout, out.at[:, span], sem_out)
    copy.start()
    copy.wait()


def first_body(weight, mine0, mine1, mine2, mine3, trailing, out, fold, cols, vin, vout, sem_in, sem_out):
    row, col, z, k = where_am_i()
    span = pl.ds(pl.multiple_of(512 * k, 512), 512)
    pltpu.make_async_copy(trailing.at[:, span], vin, sem_in).start()
    for group, ref in enumerate((mine0, mine1, mine2, mine3)):
        place(ref, 0, group, k, z, col, cols, fold)
    update(k, split(weight[...]), cols, trailing, out, vin, vout, sem_in, sem_out, row, col)


def second_body(weight, other0, others, trailing, part, half_fold, series, length, out, out_s, cols, fold, vin, vout, sem_in, sem_out):
    row, col, z, k = where_am_i()
    span = pl.ds(pl.multiple_of(512 * (1 - k), 512), 512)
    pltpu.make_async_copy(trailing.at[:, span], vin, sem_in).start()
    for at in range(16):
        rows = pl.ds(pl.multiple_of(32 * at + 16 * k, 16), 16)
        fold[rows, :] = half_fold[rows, :]
    place(other0, 0, 0, 1 - k, z, col, cols, fold)
    for group in range(1, 4):
        place(others, 544 * (group - 1), group, 1 - k, z, col, cols, fold)
    w = split(weight[...])
    correction = dot3(w, split(fold[...]), NN)
    active = row < length[...]
    correction = jnp.where(active, correction, 0.0)
    out_s[...] = series[...] - correction.T[0:64, :]
    update(1 - k, w, cols, trailing, out, vin, vout, sem_in, sem_out, row, col)


def spread_body(panel, stripe, out):
    k = lax.axis_index("row") % 2
    half = stripe[pl.ds(pl.multiple_of(16 * k, 16), 16), :]
    for c in range(16):
        out[c, 0:32, :] = panel[...]
        out[c, 32:48, :] = half


VMEM = pl.BlockSpec(memory_space=pltpu.VMEM)
ANY = pl.BlockSpec(memory_space=pl.ANY)


def shape(*dims):
    return jax.ShapeDtypeStruct(dims, jnp.float32)


def kernel(body, out, outs, memory, scratch=(), alias=None):
    def call(*args):
        args = [near_memory(a) if m == "v" else a for a, m in zip(args, memory)]
        return pl.pallas_call(
            body,
            out_shape=out,
            in_specs=[VMEM if m == "v" else ANY for m in memory],
            out_specs=outs,
            scratch_shapes=list(scratch),
            input_output_aliases=alias or {},
        )(*args)

    return call


def block(*dims):
    return pltpu.VMEM(dims, jnp.float32)


def step(trailing, panel, inv_factor, later_series, fold_series, fold_len):
    chunk = send(panel, TRANSPOSE)
    load = kernel(spread_body, shape(16, 48, 512), VMEM, "vv")(panel, inv_factor.T)
    gathered = lax.all_to_all(load, "col", 0, 0, tiled=True)
    packed = kernel(pack_body, shape(136, 128), VMEM, "vv")(chunk, fold_series)
    far = [packed] + [send(packed, shift(d)) for d in (4, -4, 8)]
    near = jnp.concatenate(far, 0)
    mine = [send(near, shift(1)), send(near, shift(-1)), send(near, PM2)]
    other0 = send(near, SWAP)
    other = send(gathered[:, 32:, :], SWAP)
    weight = kernel(weight_body, shape(512, 512), VMEM, "vv", [block(512, 512), block(512, 512)])(gathered, other)
    joined = kernel(join_body, shape(1632, 128), VMEM, "vvva")(*mine, weight)
    others = send(joined, SWAP)
    work = [block(512, 512), block(512, 512), pltpu.SemaphoreType.DMA, pltpu.SemaphoreType.DMA]
    part, half_fold = kernel(
        first_body, (shape(512, 1024), shape(512, 128)), (ANY, VMEM), "vvvvva", [block(512, 512)] + work
    )(weight, near, *mine, trailing)
    length = jnp.pad(fold_len, (0, 64))[None, :]
    out, series = kernel(
        second_body,
        (shape(512, 1024), shape(64, 512)),
        (ANY, VMEM),
        "vvvaavvv",
        [block(512, 512), block(512, 128)] + work,
        {4: 0},
    )(weight, other0, others, trailing, part, half_fold, later_series.T, length)
    return out, series.T


def solution(mesh):
    in_specs = (
        P("row", "col"),
        P(("row", "col"), None),
        P(None, "col"),
        P("row", "col"),
        P("row", "col"),
        P("col"),
    )
    out_specs = (P("row", "col"), P("row", "col"))
    return jax.shard_map(step, mesh=mesh, in_specs=in_specs, out_specs=out_specs, check_vma=False)
```

```python
import jax
import jax.numpy as jnp
from jax import lax
from jax.experimental import pallas as pl
from jax.experimental.pallas import tpu as pltpu
from jax.sharding import PartitionSpec as P


AXES = ("row", "col")
X, Y, Z, CORES = 4, 4, 16, 2
NT = (((1,), (1,)), ((), ()))
NN = (((1,), (0,)), ((), ()))


def device(x, y, z, k):
    return ((z % Z) * CORES + k) * (X * Y) + (x % X) * Y + y % Y


def pairs(move):
    out = []
    for x in range(X):
        for y in range(Y):
            for z in range(Z):
                for k in range(CORES):
                    out.append((device(x, y, z, k), device(*move(x, y, z, k))))
    return out


STEPS = {
    8: (0, 0),
    7: (1, 0), 9: (3, 0), 6: (0, 1), 10: (0, 3),
    5: (1, 1), 11: (1, 3), 4: (3, 1), 12: (3, 3), 3: (2, 0), 13: (0, 2),
    2: (2, 1), 14: (2, 3), 1: (1, 2), 15: (3, 2),
    0: (2, 2),
}
PLACES = {place: step for step, place in STEPS.items()}


def table(axis):
    bits = sum(STEPS[step][axis] << (2 * step) for step in range(Z))
    return bits - (1 << 32) if bits >> 31 else bits


TABLE_X, TABLE_Y = table(0), table(1)


def transpose_move(x, y, z, k):
    cx, cy = z // Y, z % Y
    return cx, cy, z + PLACES[(x - cx) % X, (y - cy) % Y], k


TRANSPOSE = pairs(transpose_move)
SWAP = pairs(lambda x, y, z, k: (x, y, z, 1 - k))
PM2 = pairs(lambda x, y, z, k: (x, y, z + 2 if k == 0 else z - 2, k))


def shift(d):
    return pairs(lambda x, y, z, k: (x, y, z + d, k))


def send(array, moves):
    return lax.ppermute(array, AXES, moves)


def split(x):
    high = x.astype(jnp.bfloat16)
    return high, (x - high.astype(jnp.float32)).astype(jnp.bfloat16)


def dot3(a, b, dims):
    ah, al = a
    bh, bl = b
    dot = lambda u, v: lax.dot_general(u, v, dims, preferred_element_type=jnp.float32)
    return dot(ah, bh) + (dot(ah, bl) + dot(al, bh))


def pack_body(chunk, fold, out):
    for j in range(4):
        out[32 * j:32 * j + 32, :] = chunk[:, 128 * j:128 * j + 128]
    out[128:136, 0:64] = fold[0:8, :]
    out[128:136, 64:128] = fold[8:16, :]


def weight_body(gathered, other, out_high, out_low, rows, inv, sems):
    k = lax.axis_index("row") % 2
    copies = [
        pltpu.make_async_copy(gathered.at[:, 0:32, :], rows, sems.at[0]),
        pltpu.make_async_copy(gathered.at[:, 32:48, :], inv.at[:, k], sems.at[1]),
        pltpu.make_async_copy(other, inv.at[:, 1 - k], sems.at[2]),
    ]
    for copy in copies:
        copy.start()
    for copy in copies:
        copy.wait()
    inverse = split(inv[...].reshape(512, 512))
    solved = dot3(split(rows[...].reshape(512, 512)), inverse, NN)
    high, low = split(dot3(split(solved), inverse, NT))
    out_high[...] = high
    out_low[...] = low


OFFSETS = (0, -4, 4, 8)


def where_am_i():
    row = lax.axis_index("row")
    return row, lax.axis_index("col"), row // 2, row % 2


def place(ref, group, core, z, col, high, low, fold):
    for slot in range(4):
        step = OFFSETS[slot]
        far = (0, -1, 1)[group] + step if group < 3 else step - 2 + 4 * core
        at = (z + far + 32) & 15
        hop = 2 * ((at - col) & 15)
        px = (col // 4 + (jnp.int32(TABLE_X) >> hop)) & 3
        py = (col + (jnp.int32(TABLE_Y) >> hop)) & 3
        rows = pl.ds(pl.multiple_of(32 * (4 * px + py), 32), 32)
        start = 544 * group + 136 * slot
        for j in range(4):
            h, l = split(ref[start + 32 * j:start + 32 * j + 32, :])
            high[rows, 128 * j:128 * j + 128] = h
            low[rows, 128 * j:128 * j + 128] = l
        tile = ref[start + 128:start + 136, :]
        first = pl.multiple_of(16 * (2 * at + core), 16)
        fold[pl.ds(first, 8), :] = tile
        fold[pl.ds(first + 8, 8), :] = pltpu.roll(tile, 64, 1)


def join_body(a, b, c, after, out, sems):
    copies = [pltpu.make_async_copy(ref, out.at[544 * i:544 * i + 544, :], sems.at[i]) for i, ref in enumerate((a, b, c))]
    for copy in copies:
        copy.start()
    for copy in copies:
        copy.wait()


def update(half, w, cols, vin, vout, out, sems, row, col):
    lower = 2 * col + half <= row
    copies = []
    for n in range(2):
        part = slice(256 * n, 256 * n + 256)

        @pl.when(lower)
        def _():
            block = tuple(c[part, :] for c in cols)
            vout[:, part] = vin[:, part] - dot3(w, block, NT)

        @pl.when(jnp.logical_not(lower))
        def _():
            vout[:, part] = vin[:, part]

        span = pl.ds(pl.multiple_of(512 * half + 256 * n, 256), 256)
        copy = pltpu.make_async_copy(vout.at[:, part], out.at[:, span], sems.at[n])
        copy.start()
        copies.append(copy)
    return copies


def begin(copies):
    for copy in copies:
        copy.start()


def end(copies):
    for copy in copies:
        copy.wait()


def first_body(w_high, w_low, mine0, mine1, mine2, mine3, trailing, out, fold, stage, high, low, wh, wl, vin, vout, sems):
    row, col, z, k = where_am_i()
    span = pl.ds(pl.multiple_of(512 * k, 512), 512)
    loads = [
        pltpu.make_async_copy(ref, stage.at[544 * i:544 * i + 544, :], sems.at[i])
        for i, ref in enumerate((mine0, mine1, mine2, mine3))
    ]
    weights = [pltpu.make_async_copy(w_high, wh, sems.at[4]), pltpu.make_async_copy(w_low, wl, sems.at[5])]
    old = [pltpu.make_async_copy(trailing.at[:, span], vin, sems.at[6])]
    begin(loads + weights + old)
    for group in range(4):
        end(loads[group:group + 1])
        place(stage, group, k, z, col, high, low, fold)
    end(weights + old)
    end(update(k, (wh[...], wl[...]), (high, low), vin, vout, out, sems.at[7:9], row, col))


def second_body(w_high, w_low, other0, others, trailing, part, half_fold, series, length, out, out_s,
                stage, high, low, wh, wl, vin, vout, fold, vs, vsout, sems):
    row, col, z, k = where_am_i()
    span = pl.ds(pl.multiple_of(512 * (1 - k), 512), 512)
    loads = [
        pltpu.make_async_copy(half_fold, fold, sems.at[0]),
        pltpu.make_async_copy(other0, stage.at[0:544, :], sems.at[1]),
        pltpu.make_async_copy(others, stage.at[544:2176, :], sems.at[2]),
    ]
    weights = [pltpu.make_async_copy(w_high, wh, sems.at[3]), pltpu.make_async_copy(w_low, wl, sems.at[4])]
    old = [pltpu.make_async_copy(trailing.at[:, span], vin, sems.at[5]), pltpu.make_async_copy(series, vs, sems.at[6])]
    begin(loads + weights + old)
    end(loads[0:2])
    place(stage, 0, 1 - k, z, col, high, low, fold)
    end(loads[2:3])
    for group in range(1, 4):
        place(stage, group, 1 - k, z, col, high, low, fold)
    end(weights + old)
    w = (wh[...], wl[...])
    writes = update(1 - k, w, (high, low), vin, vout, out, sems.at[7:9], row, col)
    correction = dot3(w, split(fold[...]), NN)
    correction = jnp.where(row < length[...], correction, 0.0)
    vsout[...] = vs[...] - correction.T[0:64, :]
    last = pltpu.make_async_copy(vsout, out_s, sems.at[9])
    begin([last])
    end(writes + [last])


def spread_body(panel, stripe, out, sems):
    k = lax.axis_index("row") % 2
    half = stripe.at[pl.ds(pl.multiple_of(16 * k, 16), 16), :]
    copies = []
    for c in range(16):
        copies.append(pltpu.make_async_copy(panel, out.at[c, 0:32, :], sems.at[2 * c]))
        copies.append(pltpu.make_async_copy(half, out.at[c, 32:48, :], sems.at[2 * c + 1]))
    begin(copies)
    end(copies)


VMEM = pl.BlockSpec(memory_space=pltpu.VMEM)
ANY = pl.BlockSpec(memory_space=pl.ANY)


def shape(*dims, dtype=jnp.float32):
    return jax.ShapeDtypeStruct(dims, dtype)


def kernel(body, out, memory, outs, scratch=(), alias=None):
    specs = {"v": VMEM, "a": ANY}
    out_specs = tuple(specs[m] for m in outs) if len(outs) > 1 else specs[outs]

    def call(*args):
        return pl.pallas_call(
            body,
            out_shape=out,
            in_specs=[specs[m] for m in memory],
            out_specs=out_specs,
            scratch_shapes=list(scratch),
            input_output_aliases=alias or {},
        )(*args)

    return call


def block(*dims, dtype=jnp.float32):
    return pltpu.VMEM(dims, dtype)


def sems(n):
    return pltpu.SemaphoreType.DMA((n,))


def step(trailing, panel, inv_factor, later_series, fold_series, fold_len):
    half = jnp.bfloat16
    chunk = send(panel, TRANSPOSE)
    load = kernel(spread_body, shape(16, 48, 512), "aa", "a", [sems(32)])(panel, inv_factor.T)
    gathered = lax.all_to_all(load, "col", 0, 0, tiled=True)
    packed = kernel(pack_body, shape(136, 128), "vv", "v")(chunk, fold_series)
    far = [packed] + [send(packed, shift(d)) for d in (4, -4, 8)]
    near = jnp.concatenate(far, 0)
    mine = [send(near, shift(1)), send(near, shift(-1)), send(near, PM2)]
    other0 = send(near, SWAP)
    other = send(gathered[:, 32:, :], SWAP)
    weight = kernel(
        weight_body,
        (shape(512, 512, dtype=half), shape(512, 512, dtype=half)),
        "aa",
        "vv",
        [block(16, 32, 512), block(16, 2, 16, 512), sems(3)],
    )(gathered, other)
    joined = kernel(join_body, shape(1632, 128), "aaaa", "a", [sems(3)])(*mine, weight[0])
    others = send(joined, SWAP)
    square = block(512, 512, dtype=half)
    work = [block(2176, 128), square, square, square, square, block(512, 512), block(512, 512)]
    part, half_fold = kernel(
        first_body, (shape(512, 1024), shape(512, 128)), "aaaaaaa", "av", work + [sems(9)]
    )(*weight, near, *mine, trailing)
    length = jnp.pad(fold_len, (0, 64))[None, :]
    out, series = kernel(
        second_body,
        (shape(512, 1024), shape(64, 512)),
        "aaaaaaaav",
        "aa",
        work + [block(512, 128), block(64, 512), block(64, 512), sems(10)],
        {5: 0},
    )(*weight, other0, others, trailing, part, half_fold, later_series.T, length)
    return out, series.T


def solution(mesh):
    in_specs = (
        P("row", "col"),
        P(("row", "col"), None),
        P(None, "col"),
        P("row", "col"),
        P("row", "col"),
        P("col"),
    )
    out_specs = (P("row", "col"), P("row", "col"))
    return jax.shard_map(step, mesh=mesh, in_specs=in_specs, out_specs=out_specs, check_vma=False)
```

```python
import jax
import jax.numpy as jnp
from jax import lax
from jax.experimental import pallas as pl
from jax.experimental.pallas import tpu as pltpu
from jax.sharding import PartitionSpec as P


AXES = ("row", "col")
X, Y, Z, CORES = 4, 4, 16, 2
NT = (((1,), (1,)), ((), ()))
NN = (((1,), (0,)), ((), ()))


def device(x, y, z, k):
    return ((z % Z) * CORES + k) * (X * Y) + (x % X) * Y + y % Y


def pairs(move):
    out = []
    for x in range(X):
        for y in range(Y):
            for z in range(Z):
                for k in range(CORES):
                    out.append((device(x, y, z, k), device(*move(x, y, z, k))))
    return out


STEPS = {
    8: (0, 0),
    7: (1, 0), 9: (3, 0), 6: (0, 1), 10: (0, 3),
    5: (1, 1), 11: (1, 3), 4: (3, 1), 12: (3, 3), 3: (2, 0), 13: (0, 2),
    2: (2, 1), 14: (2, 3), 1: (1, 2), 15: (3, 2),
    0: (2, 2),
}
PLACES = {place: step for step, place in STEPS.items()}


def table(axis):
    bits = sum(STEPS[step][axis] << (2 * step) for step in range(Z))
    return bits - (1 << 32) if bits >> 31 else bits


TABLE_X, TABLE_Y = table(0), table(1)


def transpose_move(x, y, z, k):
    cx, cy = z // Y, z % Y
    return cx, cy, z + PLACES[(x - cx) % X, (y - cy) % Y], k


TRANSPOSE = pairs(transpose_move)
SWAP = pairs(lambda x, y, z, k: (x, y, z, 1 - k))
PM2 = pairs(lambda x, y, z, k: (x, y, z + 2 if k == 0 else z - 2, k))


def shift(d):
    return pairs(lambda x, y, z, k: (x, y, z + d, k))


def send(array, moves):
    return lax.ppermute(array, AXES, moves)


def split(x):
    high = x.astype(jnp.bfloat16)
    return high, (x - high.astype(jnp.float32)).astype(jnp.bfloat16)


def dot3(a, b, dims):
    ah, al = a
    bh, bl = b
    dot = lambda u, v: lax.dot_general(u, v, dims, preferred_element_type=jnp.float32)
    return dot(ah, bh) + (dot(ah, bl) + dot(al, bh))


def pack_body(chunk, fold, out):
    for j in range(4):
        out[32 * j:32 * j + 32, :] = chunk[:, 128 * j:128 * j + 128]
    out[128:136, 0:64] = fold[0:8, :]
    out[128:136, 64:128] = fold[8:16, :]


def weight_body(gathered, other, out_high, out_low, rows, inv, sems):
    k = lax.axis_index("row") % 2
    copies = [
        pltpu.make_async_copy(gathered.at[:, 0:32, :], rows, sems.at[0]),
        pltpu.make_async_copy(gathered.at[:, 32:48, :], inv.at[:, k], sems.at[1]),
        pltpu.make_async_copy(other, inv.at[:, 1 - k], sems.at[2]),
    ]
    for copy in copies:
        copy.start()
    for copy in copies:
        copy.wait()
    inverse = split(inv[...].reshape(512, 512))
    solved = dot3(split(rows[...].reshape(512, 512)), inverse, NN)
    high, low = split(dot3(split(solved), inverse, NT))
    out_high[...] = high
    out_low[...] = low


OFFSETS = (0, -4, 4, 8)


def where_am_i():
    row = lax.axis_index("row")
    return row, lax.axis_index("col"), row // 2, row % 2


def place(ref, group, core, z, col, high, low, fold):
    for slot in range(4):
        step = OFFSETS[slot]
        far = (0, -1, 1)[group] + step if group < 3 else step - 2 + 4 * core
        at = (z + far + 32) & 15
        hop = 2 * ((at - col) & 15)
        px = (col // 4 + (jnp.int32(TABLE_X) >> hop)) & 3
        py = (col + (jnp.int32(TABLE_Y) >> hop)) & 3
        rows = pl.ds(pl.multiple_of(32 * (4 * px + py), 32), 32)
        start = 544 * group + 136 * slot
        for j in range(4):
            h, l = split(ref[start + 32 * j:start + 32 * j + 32, :])
            high[rows, 128 * j:128 * j + 128] = h
            low[rows, 128 * j:128 * j + 128] = l
        tile = ref[start + 128:start + 136, :]
        first = pl.multiple_of(16 * (2 * at + core), 16)
        fold[pl.ds(first, 8), :] = tile
        fold[pl.ds(first + 8, 8), :] = pltpu.roll(tile, 64, 1)


def update(half, w, cols, vin, vout, out, sems, row, col):
    lower = 2 * col + half <= row
    copies = []
    for n in range(2):
        part = slice(256 * n, 256 * n + 256)

        @pl.when(lower)
        def _():
            block = tuple(c[part, :] for c in cols)
            vout[:, part] = vin[:, part] - dot3(w, block, NT)

        @pl.when(jnp.logical_not(lower))
        def _():
            vout[:, part] = vin[:, part]

        span = pl.ds(pl.multiple_of(512 * half + 256 * n, 256), 256)
        copy = pltpu.make_async_copy(vout.at[:, part], out.at[:, span], sems.at[n])
        copy.start()
        copies.append(copy)
    return copies


def begin(copies):
    for copy in copies:
        copy.start()


def end(copies):
    for copy in copies:
        copy.wait()


def first_body(w_high, w_low, mine0, mine1, mine2, mine3, trailing, out, fold, stage, high, low, wh, wl, vin, vout, sems):
    row, col, z, k = where_am_i()
    span = pl.ds(pl.multiple_of(512 * k, 512), 512)
    loads = [
        pltpu.make_async_copy(ref, stage.at[544 * i:544 * i + 544, :], sems.at[i])
        for i, ref in enumerate((mine0, mine1, mine2, mine3))
    ]
    weights = [pltpu.make_async_copy(w_high, wh, sems.at[4]), pltpu.make_async_copy(w_low, wl, sems.at[5])]
    old = [pltpu.make_async_copy(trailing.at[:, span], vin, sems.at[6])]
    begin(loads + weights + old)
    for group in range(4):
        end(loads[group:group + 1])
        place(stage, group, k, z, col, high, low, fold)
    end(weights + old)
    end(update(k, (wh[...], wl[...]), (high, low), vin, vout, out, sems.at[7:9], row, col))


def second_body(w_high, w_low, other0, others, trailing, part, half_fold, series, length, out, out_s,
                stage, high, low, wh, wl, vin, vout, fold, vs, vsout, sems):
    row, col, z, k = where_am_i()
    span = pl.ds(pl.multiple_of(512 * (1 - k), 512), 512)
    loads = [
        pltpu.make_async_copy(half_fold, fold, sems.at[0]),
        pltpu.make_async_copy(other0, stage.at[0:544, :], sems.at[1]),
        pltpu.make_async_copy(others, stage.at[544:2176, :], sems.at[2]),
    ]
    weights = [pltpu.make_async_copy(w_high, wh, sems.at[3]), pltpu.make_async_copy(w_low, wl, sems.at[4])]
    old = [pltpu.make_async_copy(trailing.at[:, span], vin, sems.at[5]), pltpu.make_async_copy(series, vs, sems.at[6])]
    begin(loads + weights + old)
    end(loads[0:2])
    place(stage, 0, 1 - k, z, col, high, low, fold)
    end(loads[2:3])
    for group in range(1, 4):
        place(stage, group, 1 - k, z, col, high, low, fold)
    end(weights + old)
    w = (wh[...], wl[...])
    writes = update(1 - k, w, (high, low), vin, vout, out, sems.at[7:9], row, col)
    correction = dot3(w, split(fold[...]), NN)
    lengths = jnp.concatenate([length[...], length[...]], 1)
    correction = jnp.where(row < lengths, correction, 0.0)
    vsout[...] = vs[...] - correction.T[0:64, :]
    last = pltpu.make_async_copy(vsout, out_s, sems.at[9])
    begin([last])
    end(writes + [last])


def spread_body(panel, stripe, out, stage, sems):
    k = lax.axis_index("row") % 2
    loads = [
        pltpu.make_async_copy(panel, stage.at[0:32, :], sems.at[16]),
        pltpu.make_async_copy(stripe.at[pl.ds(pl.multiple_of(16 * k, 16), 16), :], stage.at[32:48, :], sems.at[17]),
    ]
    begin(loads)
    end(loads)
    copies = [pltpu.make_async_copy(stage, out.at[c], sems.at[c]) for c in range(16)]
    begin(copies)
    end(copies)


VMEM = pl.BlockSpec(memory_space=pltpu.VMEM)
ANY = pl.BlockSpec(memory_space=pl.ANY)


def shape(*dims, dtype=jnp.float32):
    return jax.ShapeDtypeStruct(dims, dtype)


def kernel(body, out, memory, outs, scratch=(), alias=None):
    specs = {"v": VMEM, "a": ANY}
    out_specs = tuple(specs[m] for m in outs) if len(outs) > 1 else specs[outs]

    def call(*args):
        return pl.pallas_call(
            body,
            out_shape=out,
            in_specs=[specs[m] for m in memory],
            out_specs=out_specs,
            scratch_shapes=list(scratch),
            input_output_aliases=alias or {},
        )(*args)

    return call


def block(*dims, dtype=jnp.float32):
    return pltpu.VMEM(dims, dtype)


def sems(n):
    return pltpu.SemaphoreType.DMA((n,))


def step(trailing, panel, inv_factor, later_series, fold_series, fold_len):
    half = jnp.bfloat16
    chunk = send(panel, TRANSPOSE)
    load = kernel(spread_body, shape(16, 48, 512), "aa", "a", [block(48, 512), sems(18)])(panel, inv_factor.T)
    gathered = lax.all_to_all(load, "col", 0, 0, tiled=True)
    packed = kernel(pack_body, shape(136, 128), "vv", "v")(chunk, fold_series)
    far = [packed] + [send(packed, shift(d)) for d in (4, -4, 8)]
    near = jnp.concatenate(far, 0)
    mine = [send(near, shift(1)), send(near, shift(-1)), send(near, PM2)]
    other0 = send(near, SWAP)
    other = send(gathered[:, 32:, :], SWAP)
    weight = kernel(
        weight_body,
        (shape(512, 512, dtype=half), shape(512, 512, dtype=half)),
        "aa",
        "vv",
        [block(16, 32, 512), block(16, 2, 16, 512), sems(3)],
    )(gathered, other)
    others = send(jnp.concatenate(mine, 0), SWAP)
    square = block(512, 512, dtype=half)
    work = [block(2176, 128), square, square, square, square, block(512, 512), block(512, 512)]
    part, half_fold = kernel(
        first_body, (shape(512, 1024), shape(512, 128)), "aaaaaaa", "av", work + [sems(9)]
    )(*weight, near, *mine, trailing)
    out, series = kernel(
        second_body,
        (shape(512, 1024), shape(64, 512)),
        "aaaaaaaav",
        "aa",
        work + [block(512, 128), block(64, 512), block(64, 512), sems(10)],
        {5: 0},
    )(*weight, other0, others, trailing, part, half_fold, later_series.T, fold_len[None, :])
    return out, series.T


def solution(mesh):
    in_specs = (
        P("row", "col"),
        P(("row", "col"), None),
        P(None, "col"),
        P("row", "col"),
        P("row", "col"),
        P("col"),
    )
    out_specs = (P("row", "col"), P("row", "col"))
    return jax.shard_map(step, mesh=mesh, in_specs=in_specs, out_specs=out_specs, check_vma=False)
```

```python
import jax
import jax.numpy as jnp
from jax import lax
from jax.experimental import pallas as pl
from jax.experimental.pallas import tpu as pltpu
from jax.sharding import PartitionSpec as P


AXES = ("row", "col")
X, Y, Z, CORES = 4, 4, 16, 2
NT = (((1,), (1,)), ((), ()))
NN = (((1,), (0,)), ((), ()))


def device(x, y, z, k):
    return ((z % Z) * CORES + k) * (X * Y) + (x % X) * Y + y % Y


def pairs(move):
    out = []
    for x in range(X):
        for y in range(Y):
            for z in range(Z):
                for k in range(CORES):
                    out.append((device(x, y, z, k), device(*move(x, y, z, k))))
    return out


STEPS = {
    4: (2, 2),
    12: (2, 1), 3: (2, 3), 13: (1, 2), 5: (3, 2),
    11: (1, 1), 2: (1, 3), 14: (3, 1), 6: (3, 3), 10: (2, 0), 1: (0, 2),
    15: (1, 0), 7: (3, 0), 9: (0, 1), 0: (0, 3),
    8: (0, 0),
}
PLACES = {place: step for step, place in STEPS.items()}


def table(axis):
    bits = sum(STEPS[step][axis] << (2 * step) for step in range(Z))
    return bits - (1 << 32) if bits >> 31 else bits


TABLE_X, TABLE_Y = table(0), table(1)


def transpose_move(extra):
    def move(x, y, z, k):
        cx, cy = z // Y, z % Y
        return cx, cy, z + extra + PLACES[(x - cx) % X, (y - cy) % Y], k

    return move


TURN_A = pairs(transpose_move(0))
TURN_B = pairs(transpose_move(8))
SWAP = pairs(lambda x, y, z, k: (x, y, z, 1 - k))
PM2 = pairs(lambda x, y, z, k: (x, y, z + 2 if k == 0 else z - 2, k))


def shift(d):
    return pairs(lambda x, y, z, k: (x, y, z + d, k))


def send(array, moves):
    return lax.ppermute(array, AXES, moves)


def split(x):
    high = x.astype(jnp.bfloat16)
    return high, (x - high.astype(jnp.float32)).astype(jnp.bfloat16)


def dot3(a, b, dims):
    ah, al = a
    bh, bl = b
    dot = lambda u, v: lax.dot_general(u, v, dims, preferred_element_type=jnp.float32)
    return dot(ah, bh) + (dot(ah, bl) + dot(al, bh))


def weight_body(gathered, other, out_high, out_low, rows, inv, sems):
    k = lax.axis_index("row") % 2
    copies = [
        pltpu.make_async_copy(gathered.at[:, 0:32, :], rows, sems.at[0]),
        pltpu.make_async_copy(gathered.at[:, 32:48, :], inv.at[:, k], sems.at[1]),
        pltpu.make_async_copy(other, inv.at[:, 1 - k], sems.at[2]),
    ]
    for copy in copies:
        copy.start()
    for copy in copies:
        copy.wait()
    inverse = split(inv[...].reshape(512, 512))
    solved = dot3(split(rows[...].reshape(512, 512)), inverse, NN)
    high, low = split(dot3(split(solved), inverse, NT))
    out_high[...] = high
    out_low[...] = low


OFFSETS = (0, -4, 4, 8)
CHUNK_ROWS = (0, 136, 280, 416)
FOLD_ROWS = (128, 264, 408, 272)


def where_am_i():
    row = lax.axis_index("row")
    return row, lax.axis_index("col"), row // 2, row % 2


def place(ref, group, core, z, col, high, low, fold):
    for slot in range(4):
        step = OFFSETS[slot]
        far = (0, -1, 1)[group] + step if group < 3 else step - 2 + 4 * core
        at = (z + far + 32) & 15
        hop = 2 * ((at - col) & 15)
        px = (col // 4 + (jnp.int32(TABLE_X) >> hop)) & 3
        py = (col + (jnp.int32(TABLE_Y) >> hop)) & 3
        rows = pl.ds(pl.multiple_of(32 * (4 * px + py), 32), 32)
        start = 544 * group + CHUNK_ROWS[slot]
        for j in range(4):
            tiles = [ref[start + 8 * (4 * i + j):start + 8 * (4 * i + j) + 8, :] for i in range(4)]
            h, l = split(jnp.concatenate(tiles, 0))
            high[rows, 128 * j:128 * j + 128] = h
            low[rows, 128 * j:128 * j + 128] = l
        start = 544 * group + FOLD_ROWS[slot]
        tile = ref[start:start + 8, :]
        first = pl.multiple_of(16 * (2 * at + core), 16)
        fold[pl.ds(first, 8), :] = tile
        fold[pl.ds(first + 8, 8), :] = pltpu.roll(tile, 64, 1)


def update(half, w, cols, vin, vout, out, sems, row, col):
    lower = 2 * col + half <= row
    copies = []
    for n in range(2):
        part = slice(256 * n, 256 * n + 256)

        @pl.when(lower)
        def _():
            block = tuple(c[part, :] for c in cols)
            vout[:, part] = vin[:, part] - dot3(w, block, NT)

        @pl.when(jnp.logical_not(lower))
        def _():
            vout[:, part] = vin[:, part]

        span = pl.ds(pl.multiple_of(512 * half + 256 * n, 256), 256)
        copy = pltpu.make_async_copy(vout.at[:, part], out.at[:, span], sems.at[n])
        copy.start()
        copies.append(copy)
    return copies


def begin(copies):
    for copy in copies:
        copy.start()


def end(copies):
    for copy in copies:
        copy.wait()


def first_body(w_high, w_low, mine0, mine1, mine2, mine3, trailing, out, fold, stage, high, low, wh, wl, vin, vout, sems):
    row, col, z, k = where_am_i()
    span = pl.ds(pl.multiple_of(512 * k, 512), 512)
    loads = [
        pltpu.make_async_copy(ref, stage.at[544 * i:544 * i + 544, :], sems.at[i])
        for i, ref in enumerate((mine0, mine1, mine2, mine3))
    ]
    weights = [pltpu.make_async_copy(w_high, wh, sems.at[4]), pltpu.make_async_copy(w_low, wl, sems.at[5])]
    old = [pltpu.make_async_copy(trailing.at[:, span], vin, sems.at[6])]
    begin(loads + weights + old)
    for group in range(4):
        end(loads[group:group + 1])
        place(stage, group, k, z, col, high, low, fold)
    end(weights + old)
    end(update(k, (wh[...], wl[...]), (high, low), vin, vout, out, sems.at[7:9], row, col))


def second_body(w_high, w_low, other0, others, trailing, part, half_fold, series, length, out, out_s,
                stage, high, low, wh, wl, vin, vout, fold, vs, vsout, sems):
    row, col, z, k = where_am_i()
    span = pl.ds(pl.multiple_of(512 * (1 - k), 512), 512)
    loads = [
        pltpu.make_async_copy(half_fold, fold, sems.at[0]),
        pltpu.make_async_copy(other0, stage.at[0:544, :], sems.at[1]),
        pltpu.make_async_copy(others, stage.at[544:2176, :], sems.at[2]),
    ]
    weights = [pltpu.make_async_copy(w_high, wh, sems.at[3]), pltpu.make_async_copy(w_low, wl, sems.at[4])]
    old = [pltpu.make_async_copy(trailing.at[:, span], vin, sems.at[5]), pltpu.make_async_copy(series, vs, sems.at[6])]
    begin(loads + weights + old)
    end(loads[0:2])
    place(stage, 0, 1 - k, z, col, high, low, fold)
    end(loads[2:3])
    for group in range(1, 4):
        place(stage, group, 1 - k, z, col, high, low, fold)
    end(weights + old)
    w = (wh[...], wl[...])
    writes = update(1 - k, w, (high, low), vin, vout, out, sems.at[7:9], row, col)
    correction = dot3(w, split(fold[...]), NN)
    lengths = jnp.concatenate([length[...], length[...]], 1)
    correction = jnp.where(row < lengths, correction, 0.0)
    vsout[...] = vs[...] - correction.T[0:64, :]
    last = pltpu.make_async_copy(vsout, out_s, sems.at[9])
    begin([last])
    end(writes + [last])


def spread_body(panel, stripe, out, stage, sems):
    k = lax.axis_index("row") % 2
    loads = [
        pltpu.make_async_copy(panel, stage.at[0:32, :], sems.at[16]),
        pltpu.make_async_copy(stripe.at[pl.ds(pl.multiple_of(16 * k, 16), 16), :], stage.at[32:48, :], sems.at[17]),
    ]
    begin(loads)
    end(loads)
    copies = [pltpu.make_async_copy(stage, out.at[c], sems.at[c]) for c in range(16)]
    begin(copies)
    end(copies)


VMEM = pl.BlockSpec(memory_space=pltpu.VMEM)
ANY = pl.BlockSpec(memory_space=pl.ANY)


def shape(*dims, dtype=jnp.float32):
    return jax.ShapeDtypeStruct(dims, dtype)


def kernel(body, out, memory, outs, scratch=(), alias=None):
    specs = {"v": VMEM, "a": ANY}
    out_specs = tuple(specs[m] for m in outs) if len(outs) > 1 else specs[outs]

    def call(*args):
        return pl.pallas_call(
            body,
            out_shape=out,
            in_specs=[specs[m] for m in memory],
            out_specs=out_specs,
            scratch_shapes=list(scratch),
            input_output_aliases=alias or {},
        )(*args)

    return call


def block(*dims, dtype=jnp.float32):
    return pltpu.VMEM(dims, dtype)


def sems(n):
    return pltpu.SemaphoreType.DMA((n,))


def tile_order(chunk):
    return chunk.reshape(4, 8, 4, 128).transpose(0, 2, 1, 3).reshape(128, 128)


def step(trailing, panel, inv_factor, later_series, fold_series, fold_len):
    half = jnp.bfloat16
    chunk_a = tile_order(send(panel, TURN_A))
    load = kernel(spread_body, shape(16, 48, 512), "aa", "a", [block(48, 512), sems(18)])(panel, inv_factor.T)
    gathered = lax.all_to_all(load, "col", 0, 0, tiled=True)
    chunk_b = tile_order(send(panel, TURN_B))
    fold = jnp.concatenate([fold_series[0:8], fold_series[8:16]], 1)
    fold_back = send(fold, shift(4))
    base = jnp.concatenate([chunk_a, fold], 0)
    up = send(jnp.concatenate([base, fold_back], 0), shift(4))
    down = send(base, shift(-4))
    near = jnp.concatenate([base, up, down, chunk_b], 0)
    mine = [send(near, shift(1)), send(near, shift(-1)), send(near, PM2)]
    other0 = send(near, SWAP)
    other = send(gathered[:, 32:, :], SWAP)
    weight = kernel(
        weight_body,
        (shape(512, 512, dtype=half), shape(512, 512, dtype=half)),
        "aa",
        "vv",
        [block(16, 32, 512), block(16, 2, 16, 512), sems(3)],
    )(gathered, other)
    others = send(jnp.concatenate(mine, 0), SWAP)
    square = block(512, 512, dtype=half)
    work = [block(2176, 128), square, square, square, square, block(512, 512), block(512, 512)]
    part, half_fold = kernel(
        first_body, (shape(512, 1024), shape(512, 128)), "aaaaaaa", "av", work + [sems(9)]
    )(*weight, near, *mine, trailing)
    out, series = kernel(
        second_body,
        (shape(512, 1024), shape(64, 512)),
        "aaaaaaaav",
        "aa",
        work + [block(512, 128), block(64, 512), block(64, 512), sems(10)],
        {5: 0},
    )(*weight, other0, others, trailing, part, half_fold, later_series.T, fold_len[None, :])
    return out, series.T


def solution(mesh):
    in_specs = (
        P("row", "col"),
        P(("row", "col"), None),
        P(None, "col"),
        P("row", "col"),
        P("row", "col"),
        P("col"),
    )
    out_specs = (P("row", "col"), P("row", "col"))
    return jax.shard_map(step, mesh=mesh, in_specs=in_specs, out_specs=out_specs, check_vma=False)
```

```python
import jax
import jax.numpy as jnp
from jax import lax
from jax.experimental import pallas as pl
from jax.experimental.pallas import tpu as pltpu
from jax.sharding import PartitionSpec as P


AXES = ("row", "col")
X, Y, Z, CORES = 4, 4, 16, 2
NT = (((1,), (1,)), ((), ()))
NN = (((1,), (0,)), ((), ()))


def device(x, y, z, k):
    return ((z % Z) * CORES + k) * (X * Y) + (x % X) * Y + y % Y


def pairs(move):
    out = []
    for x in range(X):
        for y in range(Y):
            for z in range(Z):
                for k in range(CORES):
                    out.append((device(x, y, z, k), device(*move(x, y, z, k))))
    return out


STEPS = {
    8: (0, 0),
    7: (1, 0), 9: (3, 0), 6: (0, 1), 10: (0, 3),
    5: (1, 1), 11: (1, 3), 4: (3, 1), 12: (3, 3), 3: (2, 0), 13: (0, 2),
    2: (2, 1), 14: (2, 3), 1: (1, 2), 15: (3, 2),
    0: (2, 2),
}
PLACES = {place: step for step, place in STEPS.items()}


def table(axis):
    bits = sum(STEPS[step][axis] << (2 * step) for step in range(Z))
    return bits - (1 << 32) if bits >> 31 else bits


TABLE_X, TABLE_Y = table(0), table(1)


def transpose_move(x, y, z, k):
    cx, cy = z // Y, z % Y
    return cx, cy, z + PLACES[(x - cx) % X, (y - cy) % Y], k


TURN = pairs(transpose_move)
SWAP = pairs(lambda x, y, z, k: (x, y, z, 1 - k))
PM2 = pairs(lambda x, y, z, k: (x, y, z + 2 if k == 0 else z - 2, k))


def shift(d):
    return pairs(lambda x, y, z, k: (x, y, z + d, k))


def send(array, moves):
    return lax.ppermute(array, AXES, moves)


def split(x):
    high = x.astype(jnp.bfloat16)
    return high, (x - high.astype(jnp.float32)).astype(jnp.bfloat16)


def dot3(a, b, dims):
    ah, al = a
    bh, bl = b
    dot = lambda u, v: lax.dot_general(u, v, dims, preferred_element_type=jnp.float32)
    return dot(ah, bh) + (dot(ah, bl) + dot(al, bh))


def weight_body(gathered, out_high, out_low, rows, inv, sems):
    copies = [
        pltpu.make_async_copy(gathered.at[:, 0:32, :], rows, sems.at[0]),
        pltpu.make_async_copy(gathered.at[:, 32:64, :], inv, sems.at[1]),
    ]
    begin(copies)
    end(copies)
    inverse = split(inv[...].reshape(512, 512))
    solved = dot3(split(rows[...].reshape(512, 512)), inverse, NN)
    high, low = split(dot3(split(solved), inverse, NT))
    out_high[...] = high
    out_low[...] = low


OFFSETS = (0, -4, 4, 8)


def where_am_i():
    row = lax.axis_index("row")
    return row, lax.axis_index("col"), row // 2, row % 2


def place(ref, group, core, z, col, high, low, fold):
    for slot in range(4):
        step = OFFSETS[slot]
        far = (0, -1, 1)[group] + step if group < 3 else step - 2 + 4 * core
        at = (z + far + 32) & 15
        hop = 2 * ((at - col) & 15)
        px = (col // 4 + (jnp.int32(TABLE_X) >> hop)) & 3
        py = (col + (jnp.int32(TABLE_Y) >> hop)) & 3
        rows = pl.ds(pl.multiple_of(32 * (4 * px + py), 32), 32)
        start = 544 * group + 136 * slot
        for j in range(4):
            tiles = [ref[start + 8 * (4 * i + j):start + 8 * (4 * i + j) + 8, :] for i in range(4)]
            h, l = split(jnp.concatenate(tiles, 0))
            high[rows, 128 * j:128 * j + 128] = h
            low[rows, 128 * j:128 * j + 128] = l
        tile = ref[start + 128:start + 136, :]
        first = pl.multiple_of(16 * (2 * at + core), 16)
        fold[pl.ds(first, 8), :] = tile
        fold[pl.ds(first + 8, 8), :] = pltpu.roll(tile, 64, 1)


def update(half, w, cols, vin, vout, out, sems, row, col):
    lower = 2 * col + half <= row
    copies = []
    for n in range(2):
        part = slice(256 * n, 256 * n + 256)

        @pl.when(lower)
        def _():
            block = tuple(c[part, :] for c in cols)
            vout[:, part] = vin[:, part] - dot3(w, block, NT)

        @pl.when(jnp.logical_not(lower))
        def _():
            vout[:, part] = vin[:, part]

        span = pl.ds(pl.multiple_of(512 * half + 256 * n, 256), 256)
        copy = pltpu.make_async_copy(vout.at[:, part], out.at[:, span], sems.at[n])
        copy.start()
        copies.append(copy)
    return copies


def begin(copies):
    for copy in copies:
        copy.start()


def end(copies):
    for copy in copies:
        copy.wait()


def first_body(w_high, w_low, mine0, mine1, mine2, mine3, trailing, out, fold, stage, high, low, wh, wl, vin, vout, sems):
    row, col, z, k = where_am_i()
    span = pl.ds(pl.multiple_of(512 * k, 512), 512)
    loads = [
        pltpu.make_async_copy(ref, stage.at[544 * i:544 * i + 544, :], sems.at[i])
        for i, ref in enumerate((mine0, mine1, mine2, mine3))
    ]
    weights = [pltpu.make_async_copy(w_high, wh, sems.at[4]), pltpu.make_async_copy(w_low, wl, sems.at[5])]
    old = [pltpu.make_async_copy(trailing.at[:, span], vin, sems.at[6])]
    begin(loads + weights + old)
    for group in range(4):
        end(loads[group:group + 1])
        place(stage, group, k, z, col, high, low, fold)
    end(weights + old)
    end(update(k, (wh[...], wl[...]), (high, low), vin, vout, out, sems.at[7:9], row, col))


def second_body(w_high, w_low, other0, others, trailing, part, half_fold, series, length, out, out_s,
                stage, high, low, wh, wl, vin, vout, fold, vs, vsout, sems):
    row, col, z, k = where_am_i()
    span = pl.ds(pl.multiple_of(512 * (1 - k), 512), 512)
    loads = [
        pltpu.make_async_copy(half_fold, fold, sems.at[0]),
        pltpu.make_async_copy(other0, stage.at[0:544, :], sems.at[1]),
        pltpu.make_async_copy(others, stage.at[544:2176, :], sems.at[2]),
    ]
    weights = [pltpu.make_async_copy(w_high, wh, sems.at[3]), pltpu.make_async_copy(w_low, wl, sems.at[4])]
    old = [pltpu.make_async_copy(trailing.at[:, span], vin, sems.at[5]), pltpu.make_async_copy(series, vs, sems.at[6])]
    begin(loads + weights + old)
    end(loads[0:2])
    place(stage, 0, 1 - k, z, col, high, low, fold)
    end(loads[2:3])
    for group in range(1, 4):
        place(stage, group, 1 - k, z, col, high, low, fold)
    end(weights + old)
    w = (wh[...], wl[...])
    writes = update(1 - k, w, (high, low), vin, vout, out, sems.at[7:9], row, col)
    correction = dot3(w, split(fold[...]), NN)
    lengths = jnp.concatenate([length[...], length[...]], 1)
    correction = jnp.where(row < lengths, correction, 0.0)
    vsout[...] = vs[...] - correction.T[0:64, :]
    last = pltpu.make_async_copy(vsout, out_s, sems.at[9])
    begin([last])
    end(writes + [last])


def spread_body(panel, stripe, out, stage, sems):
    loads = [
        pltpu.make_async_copy(panel, stage.at[0:32, :], sems.at[16]),
        pltpu.make_async_copy(stripe, stage.at[32:64, :], sems.at[17]),
    ]
    begin(loads)
    end(loads)
    copies = [pltpu.make_async_copy(stage, out.at[c], sems.at[c]) for c in range(16)]
    begin(copies)
    end(copies)


VMEM = pl.BlockSpec(memory_space=pltpu.VMEM)
ANY = pl.BlockSpec(memory_space=pl.ANY)


def shape(*dims, dtype=jnp.float32):
    return jax.ShapeDtypeStruct(dims, dtype)


def kernel(body, out, memory, outs, scratch=(), alias=None):
    specs = {"v": VMEM, "a": ANY}
    out_specs = tuple(specs[m] for m in outs) if len(outs) > 1 else specs[outs]

    def call(*args):
        return pl.pallas_call(
            body,
            out_shape=out,
            in_specs=[specs[m] for m in memory],
            out_specs=out_specs,
            scratch_shapes=list(scratch),
            input_output_aliases=alias or {},
        )(*args)

    return call


def block(*dims, dtype=jnp.float32):
    return pltpu.VMEM(dims, dtype)


def sems(n):
    return pltpu.SemaphoreType.DMA((n,))


def tile_order(chunk):
    return chunk.reshape(4, 8, 4, 128).transpose(0, 2, 1, 3).reshape(128, 128)


def step(trailing, panel, inv_factor, later_series, fold_series, fold_len):
    half = jnp.bfloat16
    chunk = tile_order(send(panel, TURN))
    load = kernel(spread_body, shape(16, 64, 512), "aa", "a", [block(64, 512), sems(18)])(panel, inv_factor.T)
    gathered = lax.all_to_all(load, "col", 0, 0, tiled=True)
    fold = jnp.concatenate([fold_series[0:8], fold_series[8:16]], 1)
    base = jnp.concatenate([chunk, fold], 0)
    near = jnp.concatenate([base] + [send(base, shift(d)) for d in (4, -4, 8)], 0)
    mine = [near, send(near, shift(1)), send(near, shift(-1)), send(near, PM2)]
    weight = kernel(
        weight_body,
        (shape(512, 512, dtype=half), shape(512, 512, dtype=half)),
        "a",
        "vv",
        [block(16, 32, 512), block(16, 32, 512), sems(2)],
    )(gathered)
    other0 = send(near, SWAP)
    others = send(jnp.concatenate(mine[1:], 0), SWAP)
    square = block(512, 512, dtype=half)
    work = [block(2176, 128), square, square, square, square, block(512, 512), block(512, 512)]
    part, half_fold = kernel(
        first_body, (shape(512, 1024), shape(512, 128)), "aaaaaaa", "av", work + [sems(9)]
    )(*weight, *mine, trailing)
    out, series = kernel(
        second_body,
        (shape(512, 1024), shape(64, 512)),
        "aaaaaaaav",
        "aa",
        work + [block(512, 128), block(64, 512), block(64, 512), sems(10)],
        {5: 0},
    )(*weight, other0, others, trailing, part, half_fold, later_series.T, fold_len[None, :])
    return out, series.T


def solution(mesh):
    in_specs = (
        P("row", "col"),
        P(("row", "col"), None),
        P(None, "col"),
        P("row", "col"),
        P("row", "col"),
        P("col"),
    )
    out_specs = (P("row", "col"), P("row", "col"))
    return jax.shard_map(step, mesh=mesh, in_specs=in_specs, out_specs=out_specs, check_vma=False)
```

```python
import jax
import jax.numpy as jnp
from jax import lax
from jax.experimental import pallas as pl
from jax.experimental.pallas import tpu as pltpu
from jax.sharding import PartitionSpec as P


AXES = ("row", "col")
X, Y, Z, CORES = 4, 4, 16, 2
NT = (((1,), (1,)), ((), ()))
NN = (((1,), (0,)), ((), ()))


def device(x, y, z, k):
    return ((z % Z) * CORES + k) * (X * Y) + (x % X) * Y + y % Y


def pairs(move):
    out = []
    for x in range(X):
        for y in range(Y):
            for z in range(Z):
                for k in range(CORES):
                    out.append((device(x, y, z, k), device(*move(x, y, z, k))))
    return out


STEPS = {
    8: (0, 0),
    7: (1, 0), 9: (3, 0), 6: (0, 1), 10: (0, 3),
    5: (1, 1), 11: (1, 3), 4: (3, 1), 12: (3, 3), 3: (2, 0), 13: (0, 2),
    2: (2, 1), 14: (2, 3), 1: (1, 2), 15: (3, 2),
    0: (2, 2),
}
PLACES = {place: step for step, place in STEPS.items()}


def table(axis):
    bits = sum(STEPS[step][axis] << (2 * step) for step in range(Z))
    return bits - (1 << 32) if bits >> 31 else bits


TABLE_X, TABLE_Y = table(0), table(1)


def transpose_move(x, y, z, k):
    cx, cy = z // Y, z % Y
    return cx, cy, z + PLACES[(x - cx) % X, (y - cy) % Y], k


TURN = pairs(transpose_move)
SWAP = pairs(lambda x, y, z, k: (x, y, z, 1 - k))
PM2 = pairs(lambda x, y, z, k: (x, y, z + 2 if k == 0 else z - 2, k))


def shift(d):
    return pairs(lambda x, y, z, k: (x, y, z + d, k))


def send(array, moves):
    return lax.ppermute(array, AXES, moves)


def fast(array):
    return pltpu.with_memory_space_constraint(array, pltpu.VMEM)


def split(x):
    high = x.astype(jnp.bfloat16)
    return high, (x - high.astype(jnp.float32)).astype(jnp.bfloat16)


def dot3(a, b, dims):
    ah, al = a
    bh, bl = b
    dot = lambda u, v: lax.dot_general(u, v, dims, preferred_element_type=jnp.float32)
    return dot(ah, bh) + (dot(ah, bl) + dot(al, bh))


def weight_body(gathered, out_high, out_low):
    inverse = split(gathered[:, 32:64, :].reshape(512, 512))
    solved = dot3(split(gathered[:, 0:32, :].reshape(512, 512)), inverse, NN)
    high, low = split(dot3(split(solved), inverse, NT))
    out_high[...] = high
    out_low[...] = low


OFFSETS = (0, -4, 4, 8)


def where_am_i():
    row = lax.axis_index("row")
    return row, lax.axis_index("col"), row // 2, row % 2


def place(ref, base, group, core, z, col, high, low, fold):
    for slot in range(4):
        step = OFFSETS[slot]
        far = (0, -1, 1)[group] + step if group < 3 else step - 2 + 4 * core
        at = (z + far + 32) & 15
        hop = 2 * ((at - col) & 15)
        px = (col // 4 + (jnp.int32(TABLE_X) >> hop)) & 3
        py = (col + (jnp.int32(TABLE_Y) >> hop)) & 3
        rows = pl.ds(pl.multiple_of(32 * (4 * px + py), 32), 32)
        start = base + 136 * slot
        for j in range(4):
            tiles = [ref[start + 8 * (4 * i + j):start + 8 * (4 * i + j) + 8, :] for i in range(4)]
            h, l = split(jnp.concatenate(tiles, 0))
            high[rows, 128 * j:128 * j + 128] = h
            low[rows, 128 * j:128 * j + 128] = l
        tile = ref[start + 128:start + 136, :]
        first = pl.multiple_of(16 * (2 * at + core), 16)
        fold[pl.ds(first, 8), :] = tile
        fold[pl.ds(first + 8, 8), :] = pltpu.roll(tile, 64, 1)


def update(half, w, cols, vin, vout, out, sems, row, col):
    lower = 2 * col + half <= row
    copies = []
    for n in range(2):
        part = slice(256 * n, 256 * n + 256)
        span = pl.ds(pl.multiple_of(512 * half + 256 * n, 256), 256)

        @pl.when(lower)
        def _():
            block = tuple(c[part, :] for c in cols)
            vout[:, part] = vin[:, span] - dot3(w, block, NT)

        @pl.when(jnp.logical_not(lower))
        def _():
            vout[:, part] = vin[:, span]

        copy = pltpu.make_async_copy(vout.at[:, part], out.at[:, span], sems.at[n])
        copy.start()
        copies.append(copy)
    return copies


def begin(copies):
    for copy in copies:
        copy.start()


def end(copies):
    for copy in copies:
        copy.wait()


def first_body(wh, wl, vin, mine0, mine1, mine2, mine3, out, fold, high, low, vout, sems):
    row, col, z, k = where_am_i()
    for group, ref in enumerate((mine0, mine1, mine2, mine3)):
        place(ref, 0, group, k, z, col, high, low, fold)
    end(update(k, (wh[...], wl[...]), (high, low), vin, vout, out, sems, row, col))


def second_body(wh, wl, vin, others, half_fold, series, length, part, out, out_s, high, low, vout, fold, vsout, sems):
    row, col, z, k = where_am_i()
    for group in range(4):
        place(others, 544 * group, group, 1 - k, z, col, high, low, fold)
    w = (wh[...], wl[...])
    writes = update(1 - k, w, (high, low), vin, vout, out, sems.at[0:2], row, col)
    for at in range(16):
        rows = pl.ds(pl.multiple_of(32 * at + 16 * k, 16), 16)
        fold[rows, :] = half_fold[rows, :]
    correction = dot3(w, split(fold[...]), NN)
    lengths = jnp.concatenate([length[...], length[...]], 1)
    correction = jnp.where(row < lengths, correction, 0.0)
    vsout[...] = series[...] - correction.T[0:64, :]
    last = pltpu.make_async_copy(vsout, out_s, sems.at[2])
    begin([last])
    end(writes + [last])


def spread_body(panel, stripe, out, stage, sems):
    loads = [
        pltpu.make_async_copy(panel, stage.at[0:32, :], sems.at[16]),
        pltpu.make_async_copy(stripe, stage.at[32:64, :], sems.at[17]),
    ]
    begin(loads)
    end(loads)
    copies = [pltpu.make_async_copy(stage, out.at[c], sems.at[c]) for c in range(16)]
    begin(copies)
    end(copies)


VMEM = pl.BlockSpec(memory_space=pltpu.VMEM)
ANY = pl.BlockSpec(memory_space=pl.ANY)


def shape(*dims, dtype=jnp.float32):
    return jax.ShapeDtypeStruct(dims, dtype)


def kernel(body, out, memory, outs, scratch=(), alias=None, room=24):
    specs = {"v": VMEM, "a": ANY}
    out_specs = tuple(specs[m] for m in outs) if len(outs) > 1 else specs[outs]
    limit = room << 20 if room else None

    def call(*args):
        args = [fast(a) if m == "v" else a for a, m in zip(args, memory)]
        return pl.pallas_call(
            body,
            out_shape=out,
            in_specs=[specs[m] for m in memory],
            out_specs=out_specs,
            scratch_shapes=list(scratch),
            input_output_aliases=alias or {},
            compiler_params=pltpu.CompilerParams(vmem_limit_bytes=limit),
        )(*args)

    return call


def block(*dims, dtype=jnp.float32):
    return pltpu.VMEM(dims, dtype)


def sems(n):
    return pltpu.SemaphoreType.DMA((n,))


def tile_order(chunk):
    return chunk.reshape(4, 8, 4, 128).transpose(0, 2, 1, 3).reshape(128, 128)


def step(trailing, panel, inv_factor, later_series, fold_series, fold_len):
    half = jnp.bfloat16
    chunk = tile_order(send(panel, TURN))
    load = kernel(
        spread_body, shape(16, 64, 512), "aa", "a", [block(64, 512), sems(18)], room=0
    )(panel, inv_factor.T)
    gathered = lax.all_to_all(load, "col", 0, 0, tiled=True)
    fold = jnp.concatenate([fold_series[0:8], fold_series[8:16]], 1)
    base = jnp.concatenate([chunk, fold], 0)
    near = jnp.concatenate([base] + [send(base, shift(d)) for d in (4, -4, 8)], 0)
    mine = [near, send(near, shift(1)), send(near, shift(-1)), send(near, PM2)]
    halves = (shape(512, 512, dtype=half), shape(512, 512, dtype=half))
    weight = kernel(weight_body, halves, "v", "vv")(gathered)
    held = lax.optimization_barrier(near)
    others = send(jnp.concatenate([held] + mine[1:], 0), SWAP)
    square = block(512, 512, dtype=half)
    work = [square, square, block(512, 512)]
    part, half_fold = kernel(
        first_body, (shape(512, 1024), shape(512, 128)), "vvvvvvv", "av", work + [sems(2)]
    )(*weight, trailing, *mine)
    out, series = kernel(
        second_body,
        (shape(512, 1024), shape(64, 512)),
        "vvvvvvva",
        "aa",
        work + [block(512, 128), block(64, 512), sems(3)],
        {7: 0},
    )(*weight, trailing, others, half_fold, later_series.T, fold_len[None, :], part)
    return out, series.T


def solution(mesh):
    in_specs = (
        P("row", "col"),
        P(("row", "col"), None),
        P(None, "col"),
        P("row", "col"),
        P("row", "col"),
        P("col"),
    )
    out_specs = (P("row", "col"), P("row", "col"))
    return jax.shard_map(step, mesh=mesh, in_specs=in_specs, out_specs=out_specs, check_vma=False)
```

```python
import jax
import jax.numpy as jnp
from jax import lax
from jax.experimental import pallas as pl
from jax.experimental.pallas import tpu as pltpu
from jax.sharding import PartitionSpec as P


AXES = ("row", "col")
X, Y, Z, CORES = 4, 4, 16, 2
NT = (((1,), (1,)), ((), ()))
NN = (((1,), (0,)), ((), ()))


def device(x, y, z, k):
    return ((z % Z) * CORES + k) * (X * Y) + (x % X) * Y + y % Y


def pairs(move):
    out = []
    for x in range(X):
        for y in range(Y):
            for z in range(Z):
                for k in range(CORES):
                    out.append((device(x, y, z, k), device(*move(x, y, z, k))))
    return out


STEPS = {
    8: (0, 0),
    7: (1, 0), 9: (3, 0), 6: (0, 1), 10: (0, 3),
    5: (1, 1), 11: (1, 3), 4: (3, 1), 12: (3, 3), 3: (2, 0), 13: (0, 2),
    2: (2, 1), 14: (2, 3), 1: (1, 2), 15: (3, 2),
    0: (2, 2),
}
PLACES = {place: step for step, place in STEPS.items()}


def table(axis):
    bits = sum(STEPS[step][axis] << (2 * step) for step in range(Z))
    return bits - (1 << 32) if bits >> 31 else bits


TABLE_X, TABLE_Y = table(0), table(1)


def transpose_move(x, y, z, k):
    cx, cy = z // Y, z % Y
    return cx, cy, z + PLACES[(x - cx) % X, (y - cy) % Y], k


TURN = pairs(transpose_move)
SWAP = pairs(lambda x, y, z, k: (x, y, z, 1 - k))


def onward(d):
    return pairs(lambda x, y, z, k: (x, y, z + d if k == 0 else z - d, k))


def send(array, moves):
    return lax.ppermute(array, AXES, moves)


def fast(array):
    return pltpu.with_memory_space_constraint(array, pltpu.VMEM)


def split(x):
    high = x.astype(jnp.bfloat16)
    return high, (x - high.astype(jnp.float32)).astype(jnp.bfloat16)


def dot3(a, b, dims):
    ah, al = a
    bh, bl = b
    dot = lambda u, v: lax.dot_general(u, v, dims, preferred_element_type=jnp.float32)
    return dot(ah, bh) + (dot(ah, bl) + dot(al, bh))


def weight_body(gathered, out_high, out_low):
    inverse = split(gathered[:, 32:64, :].reshape(512, 512))
    solved = dot3(split(gathered[:, 0:32, :].reshape(512, 512)), inverse, NN)
    high, low = split(dot3(split(solved), inverse, NT))
    out_high[...] = high
    out_low[...] = low


BEYOND = (0, -4, 4, -8)
AROUND = (0, -1, 1, -2)


def where_am_i():
    row = lax.axis_index("row")
    return row, lax.axis_index("col"), row // 2, row % 2


def place(ref, base, group, core, z, col, high, low, fold):
    for slot in range(4):
        way = 1 - 2 * core
        at = (z + way * (AROUND[group] + BEYOND[slot]) + 32) & 15
        hop = 2 * ((at - col) & 15)
        px = (col // 4 + (jnp.int32(TABLE_X) >> hop)) & 3
        py = (col + (jnp.int32(TABLE_Y) >> hop)) & 3
        rows = pl.ds(pl.multiple_of(32 * (4 * px + py), 32), 32)
        start = base + 136 * slot
        for j in range(4):
            tiles = [ref[start + 8 * (4 * i + j):start + 8 * (4 * i + j) + 8, :] for i in range(4)]
            h, l = split(jnp.concatenate(tiles, 0))
            high[rows, 128 * j:128 * j + 128] = h
            low[rows, 128 * j:128 * j + 128] = l
        tile = ref[start + 128:start + 136, :]
        first = pl.multiple_of(16 * (2 * at + core), 16)
        fold[pl.ds(first, 8), :] = tile
        fold[pl.ds(first + 8, 8), :] = pltpu.roll(tile, 64, 1)


def update(half, w, cols, vin, vout, out, sems, row, col):
    lower = 2 * col + half <= row
    copies = []
    for n in range(2):
        part = slice(256 * n, 256 * n + 256)
        span = pl.ds(pl.multiple_of(512 * half + 256 * n, 256), 256)

        @pl.when(lower)
        def _():
            block = tuple(c[part, :] for c in cols)
            vout[:, part] = vin[:, span] - dot3(w, block, NT)

        @pl.when(jnp.logical_not(lower))
        def _():
            vout[:, part] = vin[:, span]

        copy = pltpu.make_async_copy(vout.at[:, part], out.at[:, span], sems.at[n])
        copy.start()
        copies.append(copy)
    return copies


def begin(copies):
    for copy in copies:
        copy.start()


def end(copies):
    for copy in copies:
        copy.wait()


def first_body(wh, wl, vin, mine0, mine1, mine2, mine3, out, fold, high, low, vout, sems):
    row, col, z, k = where_am_i()
    for group, ref in enumerate((mine0, mine1, mine2, mine3)):
        place(ref, 0, group, k, z, col, high, low, fold)
    end(update(k, (wh[...], wl[...]), (high, low), vin, vout, out, sems, row, col))


def second_body(wh, wl, vin, others, half_fold, series, length, part, out, out_s, high, low, vout, fold, vsout, sems):
    row, col, z, k = where_am_i()
    for group in range(4):
        place(others, 544 * group, group, 1 - k, z, col, high, low, fold)
    w = (wh[...], wl[...])
    writes = update(1 - k, w, (high, low), vin, vout, out, sems.at[0:2], row, col)
    for at in range(16):
        rows = pl.ds(pl.multiple_of(32 * at + 16 * k, 16), 16)
        fold[rows, :] = half_fold[rows, :]
    correction = dot3(w, split(fold[...]), NN)
    lengths = jnp.concatenate([length[...], length[...]], 1)
    correction = jnp.where(row < lengths, correction, 0.0)
    vsout[...] = series[...] - correction.T[0:64, :]
    last = pltpu.make_async_copy(vsout, out_s, sems.at[2])
    begin([last])
    end(writes + [last])


def spread_body(panel, stripe, out, stage, sems):
    loads = [
        pltpu.make_async_copy(panel, stage.at[0:32, :], sems.at[16]),
        pltpu.make_async_copy(stripe, stage.at[32:64, :], sems.at[17]),
    ]
    begin(loads)
    end(loads)
    copies = [pltpu.make_async_copy(stage, out.at[c], sems.at[c]) for c in range(16)]
    begin(copies)
    end(copies)


VMEM = pl.BlockSpec(memory_space=pltpu.VMEM)
ANY = pl.BlockSpec(memory_space=pl.ANY)


def shape(*dims, dtype=jnp.float32):
    return jax.ShapeDtypeStruct(dims, dtype)


def kernel(body, out, memory, outs, scratch=(), alias=None, room=24):
    specs = {"v": VMEM, "a": ANY}
    out_specs = tuple(specs[m] for m in outs) if len(outs) > 1 else specs[outs]
    limit = room << 20 if room else None

    def call(*args):
        args = [fast(a) if m == "v" else a for a, m in zip(args, memory)]
        return pl.pallas_call(
            body,
            out_shape=out,
            in_specs=[specs[m] for m in memory],
            out_specs=out_specs,
            scratch_shapes=list(scratch),
            input_output_aliases=alias or {},
            compiler_params=pltpu.CompilerParams(vmem_limit_bytes=limit),
        )(*args)

    return call


def block(*dims, dtype=jnp.float32):
    return pltpu.VMEM(dims, dtype)


def sems(n):
    return pltpu.SemaphoreType.DMA((n,))


def tile_order(chunk):
    return chunk.reshape(4, 8, 4, 128).transpose(0, 2, 1, 3).reshape(128, 128)


def step(trailing, panel, inv_factor, later_series, fold_series, fold_len):
    half = jnp.bfloat16
    chunk = tile_order(send(panel, TURN))
    load = kernel(
        spread_body, shape(16, 64, 512), "aa", "a", [block(64, 512), sems(18)], room=0
    )(panel, inv_factor.T)
    gathered = lax.all_to_all(load, "col", 0, 0, tiled=True)
    fold = jnp.concatenate([fold_series[0:8], fold_series[8:16]], 1)
    base = jnp.concatenate([chunk, fold], 0)
    behind = send(base, onward(4))
    ahead = send(base, onward(-4))
    near = jnp.concatenate([base, behind, ahead, send(behind, onward(4))], 0)
    behind = send(near, onward(1))
    ahead = send(near, onward(-1))
    mine = [near, behind, ahead, send(behind, onward(1))]
    halves = (shape(512, 512, dtype=half), shape(512, 512, dtype=half))
    weight = kernel(weight_body, halves, "v", "vv")(gathered)
    held = lax.optimization_barrier(near)
    others = send(jnp.concatenate([held] + mine[1:], 0), SWAP)
    square = block(512, 512, dtype=half)
    work = [square, square, block(512, 512)]
    part, half_fold = kernel(
        first_body, (shape(512, 1024), shape(512, 128)), "vvvvvvv", "av", work + [sems(2)]
    )(*weight, trailing, *mine)
    out, series = kernel(
        second_body,
        (shape(512, 1024), shape(64, 512)),
        "vvvvvvva",
        "aa",
        work + [block(512, 128), block(64, 512), sems(3)],
        {7: 0},
    )(*weight, trailing, others, half_fold, later_series.T, fold_len[None, :], part)
    return out, series.T


def solution(mesh):
    in_specs = (
        P("row", "col"),
        P(("row", "col"), None),
        P(None, "col"),
        P("row", "col"),
        P("row", "col"),
        P("col"),
    )
    out_specs = (P("row", "col"), P("row", "col"))
    return jax.shard_map(step, mesh=mesh, in_specs=in_specs, out_specs=out_specs, check_vma=False)
```

```python
import jax
import jax.numpy as jnp
from jax import lax
from jax.experimental import pallas as pl
from jax.experimental.pallas import tpu as pltpu
from jax.sharding import PartitionSpec as P


AXES = ("row", "col")
X, Y, Z, CORES = 4, 4, 16, 2
NT = (((1,), (1,)), ((), ()))
NN = (((1,), (0,)), ((), ()))


def device(x, y, z, k):
    return ((z % Z) * CORES + k) * (X * Y) + (x % X) * Y + y % Y


def pairs(move):
    out = []
    for x in range(X):
        for y in range(Y):
            for z in range(Z):
                for k in range(CORES):
                    out.append((device(x, y, z, k), device(*move(x, y, z, k))))
    return out


STEPS = {
    8: (0, 0),
    7: (1, 0), 9: (3, 0), 6: (0, 1), 10: (0, 3),
    5: (1, 1), 11: (1, 3), 4: (3, 1), 12: (3, 3), 3: (2, 0), 13: (0, 2),
    2: (2, 1), 14: (2, 3), 1: (1, 2), 15: (3, 2),
    0: (2, 2),
}
PLACES = {place: step for step, place in STEPS.items()}


def table(axis):
    bits = sum(STEPS[step][axis] << (2 * step) for step in range(Z))
    return bits - (1 << 32) if bits >> 31 else bits


TABLE_X, TABLE_Y = table(0), table(1)


def transpose_move(x, y, z, k):
    cx, cy = z // Y, z % Y
    return cx, cy, z + PLACES[(x - cx) % X, (y - cy) % Y], k


TURN = pairs(transpose_move)
SWAP = pairs(lambda x, y, z, k: (x, y, z, 1 - k))
PM2 = pairs(lambda x, y, z, k: (x, y, z + 2 if k == 0 else z - 2, k))


def shift(d, core=None):
    every = pairs(lambda x, y, z, k: (x, y, z + d, k))
    return [p for p in every if core is None or p[0] // (X * Y) % CORES == core]


def send(array, moves):
    return lax.ppermute(array, AXES, moves)


def fast(array):
    return pltpu.with_memory_space_constraint(array, pltpu.VMEM)


def split(x):
    high = x.astype(jnp.bfloat16)
    return high, (x - high.astype(jnp.float32)).astype(jnp.bfloat16)


def dot3(a, b, dims):
    ah, al = a
    bh, bl = b
    dot = lambda u, v: lax.dot_general(u, v, dims, preferred_element_type=jnp.float32)
    return dot(ah, bh) + (dot(ah, bl) + dot(al, bh))


def weight_body(gathered, out_high, out_low):
    inverse = split(gathered[:, 32:64, :].reshape(512, 512))
    solved = dot3(split(gathered[:, 0:32, :].reshape(512, 512)), inverse, NN)
    high, low = split(dot3(split(solved), inverse, NT))
    out_high[...] = high
    out_low[...] = low


OFFSETS = (0, -4, 4, 8)


def where_am_i():
    row = lax.axis_index("row")
    return row, lax.axis_index("col"), row // 2, row % 2


def place(ref, base, group, core, z, col, high, low, fold):
    for slot in range(4):
        step = OFFSETS[slot]
        far = (0, -1, 1)[group] + step if group < 3 else step - 2 + 4 * core
        at = (z + far + 32) & 15
        hop = 2 * ((at - col) & 15)
        px = (col // 4 + (jnp.int32(TABLE_X) >> hop)) & 3
        py = (col + (jnp.int32(TABLE_Y) >> hop)) & 3
        rows = pl.ds(pl.multiple_of(32 * (4 * px + py), 32), 32)
        start = base + 136 * slot
        for j in range(4):
            tiles = [ref[start + 8 * (4 * i + j):start + 8 * (4 * i + j) + 8, :] for i in range(4)]
            h, l = split(jnp.concatenate(tiles, 0))
            high[rows, 128 * j:128 * j + 128] = h
            low[rows, 128 * j:128 * j + 128] = l
        tile = ref[start + 128:start + 136, :]
        first = pl.multiple_of(16 * (2 * at + core), 16)
        fold[pl.ds(first, 8), :] = tile
        fold[pl.ds(first + 8, 8), :] = pltpu.roll(tile, 64, 1)


def update(half, w, cols, vin, vout, out, sems, row, col):
    lower = 2 * col + half <= row
    copies = []
    for n in range(2):
        part = slice(256 * n, 256 * n + 256)
        span = pl.ds(pl.multiple_of(512 * half + 256 * n, 256), 256)

        @pl.when(lower)
        def _():
            block = tuple(c[part, :] for c in cols)
            vout[:, part] = vin[:, span] - dot3(w, block, NT)

        @pl.when(jnp.logical_not(lower))
        def _():
            vout[:, part] = vin[:, span]

        copy = pltpu.make_async_copy(vout.at[:, part], out.at[:, span], sems.at[n])
        copy.start()
        copies.append(copy)
    return copies


def begin(copies):
    for copy in copies:
        copy.start()


def end(copies):
    for copy in copies:
        copy.wait()


def first_body(wh, wl, vin, mine0, mine1, mine2, mine3, out, fold, high, low, vout, sems):
    row, col, z, k = where_am_i()
    for group, ref in enumerate((mine0, mine1, mine2, mine3)):
        place(ref, 0, group, k, z, col, high, low, fold)
    end(update(k, (wh[...], wl[...]), (high, low), vin, vout, out, sems, row, col))


def second_body(wh, wl, vin, others, half_fold, series, length, part, out, out_s, high, low, vout, fold, vsout, sems):
    row, col, z, k = where_am_i()
    for group in range(4):
        place(others, 544 * group, group, 1 - k, z, col, high, low, fold)
    w = (wh[...], wl[...])
    writes = update(1 - k, w, (high, low), vin, vout, out, sems.at[0:2], row, col)
    for at in range(16):
        rows = pl.ds(pl.multiple_of(32 * at + 16 * k, 16), 16)
        fold[rows, :] = half_fold[rows, :]
    correction = dot3(w, split(fold[...]), NN)
    lengths = jnp.concatenate([length[...], length[...]], 1)
    correction = jnp.where(row < lengths, correction, 0.0)
    vsout[...] = series[...] - correction.T[0:64, :]
    last = pltpu.make_async_copy(vsout, out_s, sems.at[2])
    begin([last])
    end(writes + [last])


def spread_body(panel, stripe, out, stage, sems):
    loads = [
        pltpu.make_async_copy(panel, stage.at[0:32, :], sems.at[16]),
        pltpu.make_async_copy(stripe, stage.at[32:64, :], sems.at[17]),
    ]
    begin(loads)
    end(loads)
    copies = [pltpu.make_async_copy(stage, out.at[c], sems.at[c]) for c in range(16)]
    begin(copies)
    end(copies)


VMEM = pl.BlockSpec(memory_space=pltpu.VMEM)
ANY = pl.BlockSpec(memory_space=pl.ANY)


def shape(*dims, dtype=jnp.float32):
    return jax.ShapeDtypeStruct(dims, dtype)


def kernel(body, out, memory, outs, scratch=(), alias=None, room=24):
    specs = {"v": VMEM, "a": ANY}
    out_specs = tuple(specs[m] for m in outs) if len(outs) > 1 else specs[outs]
    limit = room << 20 if room else None

    def call(*args):
        args = [fast(a) if m == "v" else a for a, m in zip(args, memory)]
        return pl.pallas_call(
            body,
            out_shape=out,
            in_specs=[specs[m] for m in memory],
            out_specs=out_specs,
            scratch_shapes=list(scratch),
            input_output_aliases=alias or {},
            compiler_params=pltpu.CompilerParams(vmem_limit_bytes=limit),
        )(*args)

    return call


def block(*dims, dtype=jnp.float32):
    return pltpu.VMEM(dims, dtype)


def sems(n):
    return pltpu.SemaphoreType.DMA((n,))


def tile_order(chunk):
    return chunk.reshape(4, 8, 4, 128).transpose(0, 2, 1, 3).reshape(128, 128)


def step(trailing, panel, inv_factor, later_series, fold_series, fold_len):
    half = jnp.bfloat16
    chunk = tile_order(send(panel, TURN))
    load = kernel(
        spread_body, shape(16, 64, 512), "aa", "a", [block(64, 512), sems(18)], room=0
    )(panel, inv_factor.T)
    gathered = lax.all_to_all(load, "col", 0, 0, tiled=True)
    fold = jnp.concatenate([fold_series[0:8], fold_series[8:16]], 1)
    base = jnp.concatenate([chunk, fold], 0)
    across = send(base, shift(8, 0))
    ahead = send(base, shift(-4))
    behind = send(base, shift(4))
    across = across + send(ahead, shift(-4, 1))
    near = jnp.concatenate([base, behind, ahead, across], 0)
    mine = [near, send(near, shift(1)), send(near, shift(-1)), send(near, PM2)]
    halves = (shape(512, 512, dtype=half), shape(512, 512, dtype=half))
    weight = kernel(weight_body, halves, "v", "vv")(gathered)
    held = lax.optimization_barrier(near)
    others = send(jnp.concatenate([held] + mine[1:], 0), SWAP)
    square = block(512, 512, dtype=half)
    work = [square, square, block(512, 512)]
    part, half_fold = kernel(
        first_body, (shape(512, 1024), shape(512, 128)), "vvvvvvv", "av", work + [sems(2)]
    )(*weight, trailing, *mine)
    out, series = kernel(
        second_body,
        (shape(512, 1024), shape(64, 512)),
        "vvvvvvva",
        "aa",
        work + [block(512, 128), block(64, 512), sems(3)],
        {7: 0},
    )(*weight, trailing, others, half_fold, later_series.T, fold_len[None, :], part)
    return out, series.T


def solution(mesh):
    in_specs = (
        P("row", "col"),
        P(("row", "col"), None),
        P(None, "col"),
        P("row", "col"),
        P("row", "col"),
        P("col"),
    )
    out_specs = (P("row", "col"), P("row", "col"))
    return jax.shard_map(step, mesh=mesh, in_specs=in_specs, out_specs=out_specs, check_vma=False)
```

```python
import jax
import jax.numpy as jnp
from jax import lax
from jax.experimental import pallas as pl
from jax.experimental.pallas import tpu as pltpu
from jax.sharding import PartitionSpec as P


AXES = ("row", "col")
X, Y, Z, CORES = 4, 4, 16, 2
NT = (((1,), (1,)), ((), ()))
NN = (((1,), (0,)), ((), ()))


def device(x, y, z, k):
    return ((z % Z) * CORES + k) * (X * Y) + (x % X) * Y + y % Y


def pairs(move):
    out = []
    for x in range(X):
        for y in range(Y):
            for z in range(Z):
                for k in range(CORES):
                    out.append((device(x, y, z, k), device(*move(x, y, z, k))))
    return out


STEPS = {
    8: (0, 0),
    7: (1, 0), 9: (3, 0), 6: (0, 1), 10: (0, 3),
    5: (1, 1), 11: (1, 3), 4: (3, 1), 12: (3, 3), 3: (2, 0), 13: (0, 2),
    2: (2, 1), 14: (2, 3), 1: (1, 2), 15: (3, 2),
    0: (2, 2),
}
PLACES = {place: step for step, place in STEPS.items()}


def table(axis):
    bits = sum(STEPS[step][axis] << (2 * step) for step in range(Z))
    return bits - (1 << 32) if bits >> 31 else bits


TABLE_X, TABLE_Y = table(0), table(1)


def transpose_move(x, y, z, k):
    cx, cy = z // Y, z % Y
    return cx, cy, z + PLACES[(x - cx) % X, (y - cy) % Y], k


TURN = pairs(transpose_move)
SWAP = pairs(lambda x, y, z, k: (x, y, z, 1 - k))
PM2 = pairs(lambda x, y, z, k: (x, y, z + 2 if k == 0 else z - 2, k))


def shift(d):
    return pairs(lambda x, y, z, k: (x, y, z + d, k))


def onward(d):
    return pairs(lambda x, y, z, k: (x, y, z + d if k == 0 else z - d, k))


def send(array, moves):
    return lax.ppermute(array, AXES, moves)


def fast(array):
    return pltpu.with_memory_space_constraint(array, pltpu.VMEM)


def split(x):
    high = x.astype(jnp.bfloat16)
    return high, (x - high.astype(jnp.float32)).astype(jnp.bfloat16)


def dot3(a, b, dims):
    ah, al = a
    bh, bl = b
    dot = lambda u, v: lax.dot_general(u, v, dims, preferred_element_type=jnp.float32)
    return dot(ah, bh) + (dot(ah, bl) + dot(al, bh))


def weight_body(gathered, out_high, out_low):
    inverse = split(gathered[:, 32:64, :].reshape(512, 512))
    solved = dot3(split(gathered[:, 0:32, :].reshape(512, 512)), inverse, NN)
    high, low = split(dot3(split(solved), inverse, NT))
    out_high[...] = high
    out_low[...] = low


BEYOND = (0, -4, 4, -8)


def where_am_i():
    row = lax.axis_index("row")
    return row, lax.axis_index("col"), row // 2, row % 2


def place(ref, base, group, core, z, col, high, low, fold):
    for slot in range(4):
        way = 1 - 2 * core
        near = (0, -1, 1)[group] if group < 3 else -2 * way
        at = (z + near + way * BEYOND[slot] + 32) & 15
        hop = 2 * ((at - col) & 15)
        px = (col // 4 + (jnp.int32(TABLE_X) >> hop)) & 3
        py = (col + (jnp.int32(TABLE_Y) >> hop)) & 3
        rows = pl.ds(pl.multiple_of(32 * (4 * px + py), 32), 32)
        start = base + 136 * slot
        for j in range(4):
            tiles = [ref[start + 8 * (4 * i + j):start + 8 * (4 * i + j) + 8, :] for i in range(4)]
            h, l = split(jnp.concatenate(tiles, 0))
            high[rows, 128 * j:128 * j + 128] = h
            low[rows, 128 * j:128 * j + 128] = l
        tile = ref[start + 128:start + 136, :]
        first = pl.multiple_of(16 * (2 * at + core), 16)
        fold[pl.ds(first, 8), :] = tile
        fold[pl.ds(first + 8, 8), :] = pltpu.roll(tile, 64, 1)


def update(half, w, cols, vin, vout, out, sems, row, col):
    lower = 2 * col + half <= row
    copies = []
    for n in range(2):
        part = slice(256 * n, 256 * n + 256)
        span = pl.ds(pl.multiple_of(512 * half + 256 * n, 256), 256)

        @pl.when(lower)
        def _():
            block = tuple(c[part, :] for c in cols)
            vout[:, part] = vin[:, span] - dot3(w, block, NT)

        @pl.when(jnp.logical_not(lower))
        def _():
            vout[:, part] = vin[:, span]

        copy = pltpu.make_async_copy(vout.at[:, part], out.at[:, span], sems.at[n])
        copy.start()
        copies.append(copy)
    return copies


def begin(copies):
    for copy in copies:
        copy.start()


def end(copies):
    for copy in copies:
        copy.wait()


def first_body(wh, wl, vin, mine0, mine1, mine2, mine3, out, fold, high, low, vout, sems):
    row, col, z, k = where_am_i()
    for group, ref in enumerate((mine0, mine1, mine2, mine3)):
        place(ref, 0, group, k, z, col, high, low, fold)
    end(update(k, (wh[...], wl[...]), (high, low), vin, vout, out, sems, row, col))


def second_body(wh, wl, vin, others, half_fold, series, length, part, out, out_s, high, low, vout, fold, vsout, sems):
    row, col, z, k = where_am_i()
    for group in range(4):
        place(others, 544 * group, group, 1 - k, z, col, high, low, fold)
    w = (wh[...], wl[...])
    writes = update(1 - k, w, (high, low), vin, vout, out, sems.at[0:2], row, col)
    for at in range(16):
        rows = pl.ds(pl.multiple_of(32 * at + 16 * k, 16), 16)
        fold[rows, :] = half_fold[rows, :]
    correction = dot3(w, split(fold[...]), NN)
    lengths = jnp.concatenate([length[...], length[...]], 1)
    correction = jnp.where(row < lengths, correction, 0.0)
    vsout[...] = series[...] - correction.T[0:64, :]
    last = pltpu.make_async_copy(vsout, out_s, sems.at[2])
    begin([last])
    end(writes + [last])


def spread_body(panel, stripe, out, stage, sems):
    loads = [
        pltpu.make_async_copy(panel, stage.at[0:32, :], sems.at[16]),
        pltpu.make_async_copy(stripe, stage.at[32:64, :], sems.at[17]),
    ]
    begin(loads)
    end(loads)
    copies = [pltpu.make_async_copy(stage, out.at[c], sems.at[c]) for c in range(16)]
    begin(copies)
    end(copies)


VMEM = pl.BlockSpec(memory_space=pltpu.VMEM)
ANY = pl.BlockSpec(memory_space=pl.ANY)


def shape(*dims, dtype=jnp.float32):
    return jax.ShapeDtypeStruct(dims, dtype)


def kernel(body, out, memory, outs, scratch=(), alias=None, room=24):
    specs = {"v": VMEM, "a": ANY}
    out_specs = tuple(specs[m] for m in outs) if len(outs) > 1 else specs[outs]
    limit = room << 20 if room else None

    def call(*args):
        args = [fast(a) if m == "v" else a for a, m in zip(args, memory)]
        return pl.pallas_call(
            body,
            out_shape=out,
            in_specs=[specs[m] for m in memory],
            out_specs=out_specs,
            scratch_shapes=list(scratch),
            input_output_aliases=alias or {},
            compiler_params=pltpu.CompilerParams(vmem_limit_bytes=limit),
        )(*args)

    return call


def block(*dims, dtype=jnp.float32):
    return pltpu.VMEM(dims, dtype)


def sems(n):
    return pltpu.SemaphoreType.DMA((n,))


def tile_order(chunk):
    return chunk.reshape(4, 8, 4, 128).transpose(0, 2, 1, 3).reshape(128, 128)


def step(trailing, panel, inv_factor, later_series, fold_series, fold_len):
    half = jnp.bfloat16
    chunk = tile_order(send(panel, TURN))
    load = kernel(
        spread_body, shape(16, 64, 512), "aa", "a", [block(64, 512), sems(18)], room=0
    )(panel, inv_factor.T)
    gathered = lax.all_to_all(load, "col", 0, 0, tiled=True)
    fold = jnp.concatenate([fold_series[0:8], fold_series[8:16]], 1)
    base = jnp.concatenate([chunk, fold], 0)
    behind = send(base, onward(4))
    ahead = send(base, onward(-4))
    near = jnp.concatenate([base, behind, ahead, send(behind, onward(4))], 0)
    mine = [near, send(near, shift(1)), send(near, shift(-1)), send(near, PM2)]
    halves = (shape(512, 512, dtype=half), shape(512, 512, dtype=half))
    weight = kernel(weight_body, halves, "v", "vv")(gathered)
    held = lax.optimization_barrier(near)
    others = send(jnp.concatenate([held] + mine[1:], 0), SWAP)
    square = block(512, 512, dtype=half)
    work = [square, square, block(512, 512)]
    part, half_fold = kernel(
        first_body, (shape(512, 1024), shape(512, 128)), "vvvvvvv", "av", work + [sems(2)]
    )(*weight, trailing, *mine)
    out, series = kernel(
        second_body,
        (shape(512, 1024), shape(64, 512)),
        "vvvvvvva",
        "aa",
        work + [block(512, 128), block(64, 512), sems(3)],
        {7: 0},
    )(*weight, trailing, others, half_fold, later_series.T, fold_len[None, :], part)
    return out, series.T


def solution(mesh):
    in_specs = (
        P("row", "col"),
        P(("row", "col"), None),
        P(None, "col"),
        P("row", "col"),
        P("row", "col"),
        P("col"),
    )
    out_specs = (P("row", "col"), P("row", "col"))
    return jax.shard_map(step, mesh=mesh, in_specs=in_specs, out_specs=out_specs, check_vma=False)
```

```python
import jax
import jax.numpy as jnp
from jax import lax
from jax.experimental import pallas as pl
from jax.experimental.pallas import tpu as pltpu
from jax.sharding import PartitionSpec as P


AXES = ("row", "col")
X, Y, Z, CORES = 4, 4, 16, 2
NT = (((1,), (1,)), ((), ()))
NN = (((1,), (0,)), ((), ()))


def device(x, y, z, k):
    return ((z % Z) * CORES + k) * (X * Y) + (x % X) * Y + y % Y


def pairs(move):
    out = []
    for x in range(X):
        for y in range(Y):
            for z in range(Z):
                for k in range(CORES):
                    out.append((device(x, y, z, k), device(*move(x, y, z, k))))
    return out


STEPS = {
    8: (0, 0),
    7: (1, 0), 9: (3, 0), 6: (0, 1), 10: (0, 3),
    5: (1, 1), 11: (1, 3), 4: (3, 1), 12: (3, 3), 3: (2, 0), 13: (0, 2),
    2: (2, 1), 14: (2, 3), 1: (1, 2), 15: (3, 2),
    0: (2, 2),
}
PLACES = {place: step for step, place in STEPS.items()}


def table(axis):
    bits = sum(STEPS[step][axis] << (2 * step) for step in range(Z))
    return bits - (1 << 32) if bits >> 31 else bits


TABLE_X, TABLE_Y = table(0), table(1)


def transpose_move(x, y, z, k):
    cx, cy = z // Y, z % Y
    return cx, cy, z + PLACES[(x - cx) % X, (y - cy) % Y], k


TURN = pairs(transpose_move)
SWAP = pairs(lambda x, y, z, k: (x, y, z, 1 - k))
PM2 = pairs(lambda x, y, z, k: (x, y, z + 2 if k == 0 else z - 2, k))


def shift(d, core=None):
    every = pairs(lambda x, y, z, k: (x, y, z + d, k))
    return [p for p in every if core is None or p[0] // (X * Y) % CORES == core]


def send(array, moves):
    return lax.ppermute(array, AXES, moves)


def fast(array):
    return pltpu.with_memory_space_constraint(array, pltpu.VMEM)


def split(x):
    high = x.astype(jnp.bfloat16)
    return high, (x - high.astype(jnp.float32)).astype(jnp.bfloat16)


def dot3(a, b, dims):
    ah, al = a
    bh, bl = b
    dot = lambda u, v: lax.dot_general(u, v, dims, preferred_element_type=jnp.float32)
    return dot(ah, bh) + (dot(ah, bl) + dot(al, bh))


def weight_body(gathered, out_high, out_low):
    inverse = split(gathered[:, 32:64, :].reshape(512, 512))
    solved = dot3(split(gathered[:, 0:32, :].reshape(512, 512)), inverse, NN)
    high, low = split(dot3(split(solved), inverse, NT))
    out_high[...] = high
    out_low[...] = low


OFFSETS = (0, -4, 4, 8)


def where_am_i():
    row = lax.axis_index("row")
    return row, lax.axis_index("col"), row // 2, row % 2


def place(ref, base, group, core, z, col, high, low, fold):
    for slot in range(4):
        step = OFFSETS[slot]
        far = (0, -1, 1)[group] + step if group < 3 else step - 2 + 4 * core
        at = (z + far + 32) & 15
        hop = 2 * ((at - col) & 15)
        px = (col // 4 + (jnp.int32(TABLE_X) >> hop)) & 3
        py = (col + (jnp.int32(TABLE_Y) >> hop)) & 3
        rows = pl.ds(pl.multiple_of(32 * (4 * px + py), 32), 32)
        start = base + 136 * slot
        for j in range(4):
            tiles = [ref[start + 8 * (4 * i + j):start + 8 * (4 * i + j) + 8, :] for i in range(4)]
            h, l = split(jnp.concatenate(tiles, 0))
            high[rows, 128 * j:128 * j + 128] = h
            low[rows, 128 * j:128 * j + 128] = l
        tile = ref[start + 128:start + 136, :]
        first = pl.multiple_of(16 * (2 * at + core), 16)
        fold[pl.ds(first, 8), :] = tile
        fold[pl.ds(first + 8, 8), :] = pltpu.roll(tile, 64, 1)


def update(half, w, cols, vin, vout, row, col, done):
    lower = 2 * col + half <= row
    for n in range(2):
        part = slice(256 * n, 256 * n + 256)
        span = pl.ds(pl.multiple_of(512 * half + 256 * n, 256), 256)

        @pl.when(lower)
        def _():
            block = tuple(c[part, :] for c in cols)
            vout[:, part] = vin[:, span] - dot3(w, block, NT)

        @pl.when(jnp.logical_not(lower))
        def _():
            vout[:, part] = vin[:, span]

        done(n, part, span)


def begin(copies):
    for copy in copies:
        copy.start()


def end(copies):
    for copy in copies:
        copy.wait()


def first_body(wh, wl, vin, mine0, mine1, mine2, mine3, out, fold, high, low):
    row, col, z, k = where_am_i()
    for group, ref in enumerate((mine0, mine1, mine2, mine3)):
        place(ref, 0, group, k, z, col, high, low, fold)
    update(k, (wh[...], wl[...]), (high, low), vin, out, row, col, lambda n, part, span: None)


def second_body(wh, wl, vin, other0, others, first, half_fold, series, length, out, out_s, high, low, vout, fold, vsout, sems):
    row, col, z, k = where_am_i()
    writes = [pltpu.make_async_copy(first, out.at[:, pl.ds(pl.multiple_of(512 * k, 512), 512)], sems.at[3])]
    begin(writes)
    place(other0, 0, 0, 1 - k, z, col, high, low, fold)
    for group in range(1, 4):
        place(others, 544 * (group - 1), group, 1 - k, z, col, high, low, fold)
    w = (wh[...], wl[...])

    def done(n, part, span):
        copy = pltpu.make_async_copy(vout.at[:, part], out.at[:, span], sems.at[n])
        copy.start()
        writes.append(copy)

    update(1 - k, w, (high, low), vin, vout, row, col, done)
    for at in range(16):
        rows = pl.ds(pl.multiple_of(32 * at + 16 * k, 16), 16)
        fold[rows, :] = half_fold[rows, :]
    correction = dot3(w, split(fold[...]), NN)
    lengths = jnp.concatenate([length[...], length[...]], 1)
    correction = jnp.where(row < lengths, correction, 0.0)
    vsout[...] = series[...] - correction.T[0:64, :]
    last = pltpu.make_async_copy(vsout, out_s, sems.at[2])
    begin([last])
    end(writes + [last])


def spread_body(panel, stripe, out, stage, sems):
    loads = [
        pltpu.make_async_copy(panel, stage.at[0:32, :], sems.at[16]),
        pltpu.make_async_copy(stripe, stage.at[32:64, :], sems.at[17]),
    ]
    begin(loads)
    end(loads)
    copies = [pltpu.make_async_copy(stage, out.at[c], sems.at[c]) for c in range(16)]
    begin(copies)
    end(copies)


VMEM = pl.BlockSpec(memory_space=pltpu.VMEM)
ANY = pl.BlockSpec(memory_space=pl.ANY)


def shape(*dims, dtype=jnp.float32):
    return jax.ShapeDtypeStruct(dims, dtype)


def kernel(body, out, memory, outs, scratch=(), alias=None, room=24):
    specs = {"v": VMEM, "a": ANY}
    out_specs = tuple(specs[m] for m in outs) if len(outs) > 1 else specs[outs]
    limit = room << 20 if room else None

    def call(*args):
        args = [fast(a) if m == "v" else a for a, m in zip(args, memory)]
        return pl.pallas_call(
            body,
            out_shape=out,
            in_specs=[specs[m] for m in memory],
            out_specs=out_specs,
            scratch_shapes=list(scratch),
            input_output_aliases=alias or {},
            compiler_params=pltpu.CompilerParams(vmem_limit_bytes=limit),
        )(*args)

    return call


def block(*dims, dtype=jnp.float32):
    return pltpu.VMEM(dims, dtype)


def sems(n):
    return pltpu.SemaphoreType.DMA((n,))


def tile_order(chunk):
    return chunk.reshape(4, 8, 4, 128).transpose(0, 2, 1, 3).reshape(128, 128)


def step(trailing, panel, inv_factor, later_series, fold_series, fold_len):
    half = jnp.bfloat16
    chunk = tile_order(send(panel, TURN))
    load = kernel(
        spread_body, shape(16, 64, 512), "aa", "a", [block(64, 512), sems(18)], room=0
    )(panel, inv_factor.T)
    gathered = lax.all_to_all(load, "col", 0, 0, tiled=True)
    fold = jnp.concatenate([fold_series[0:8], fold_series[8:16]], 1)
    base = jnp.concatenate([chunk, fold], 0)
    across = send(base, shift(8, 0))
    ahead = send(base, shift(-4))
    behind = send(base, shift(4))
    across = across + send(ahead, shift(-4, 1))
    near = jnp.concatenate([base, behind, ahead, across], 0)
    mine = [near, send(near, shift(1)), send(near, shift(-1)), send(near, PM2)]
    halves = (shape(512, 512, dtype=half), shape(512, 512, dtype=half))
    weight = kernel(weight_body, halves, "v", "vv")(gathered)
    other0 = send(near, SWAP)
    others = send(jnp.concatenate(mine[1:], 0), SWAP)
    square = block(512, 512, dtype=half)
    part, half_fold = kernel(
        first_body, (shape(512, 512), shape(512, 128)), "vvvvvvv", "vv", [square, square]
    )(*weight, trailing, *mine)
    out, series = kernel(
        second_body,
        (shape(512, 1024), shape(64, 512)),
        "vvvvvvvvv",
        "aa",
        [square, square, block(512, 512), block(512, 128), block(64, 512), sems(4)],
    )(*weight, trailing, other0, others, part, half_fold, later_series.T, fold_len[None, :])
    return out, series.T


def solution(mesh):
    in_specs = (
        P("row", "col"),
        P(("row", "col"), None),
        P(None, "col"),
        P("row", "col"),
        P("row", "col"),
        P("col"),
    )
    out_specs = (P("row", "col"), P("row", "col"))
    return jax.shard_map(step, mesh=mesh, in_specs=in_specs, out_specs=out_specs, check_vma=False)
```

```python
import jax
import jax.numpy as jnp
from jax import lax
from jax.experimental import pallas as pl
from jax.experimental.pallas import tpu as pltpu
from jax.sharding import PartitionSpec as P


AXES = ("row", "col")
X, Y, Z, CORES = 4, 4, 16, 2
NT = (((1,), (1,)), ((), ()))
NN = (((1,), (0,)), ((), ()))


def device(x, y, z, k):
    return ((z % Z) * CORES + k) * (X * Y) + (x % X) * Y + y % Y


def pairs(move):
    out = []
    for x in range(X):
        for y in range(Y):
            for z in range(Z):
                for k in range(CORES):
                    out.append((device(x, y, z, k), device(*move(x, y, z, k))))
    return out


STEPS = {
    8: (0, 0),
    7: (1, 0), 9: (3, 0), 6: (0, 1), 10: (0, 3),
    5: (1, 1), 11: (1, 3), 4: (3, 1), 12: (3, 3), 3: (2, 0), 13: (0, 2),
    2: (2, 1), 14: (2, 3), 1: (1, 2), 15: (3, 2),
    0: (2, 2),
}
PLACES = {place: step for step, place in STEPS.items()}


def table(axis):
    bits = sum(STEPS[step][axis] << (2 * step) for step in range(Z))
    return bits - (1 << 32) if bits >> 31 else bits


TABLE_X, TABLE_Y = table(0), table(1)


def transpose_move(x, y, z, k):
    cx, cy = z // Y, z % Y
    return cx, cy, z + PLACES[(x - cx) % X, (y - cy) % Y], k


TURN = pairs(transpose_move)
SWAP = pairs(lambda x, y, z, k: (x, y, z, 1 - k))
PM2 = pairs(lambda x, y, z, k: (x, y, z + 2 if k == 0 else z - 2, k))


def shift(d, core=None):
    every = pairs(lambda x, y, z, k: (x, y, z + d, k))
    return [p for p in every if core is None or p[0] // (X * Y) % CORES == core]


def send(array, moves):
    return lax.ppermute(array, AXES, moves)


def fast(array):
    return pltpu.with_memory_space_constraint(array, pltpu.VMEM)


def split(x):
    high = x.astype(jnp.bfloat16)
    return high, (x - high.astype(jnp.float32)).astype(jnp.bfloat16)


def dot3(a, b, dims):
    ah, al = a
    bh, bl = b
    dot = lambda u, v: lax.dot_general(u, v, dims, preferred_element_type=jnp.float32)
    return dot(ah, bh) + (dot(ah, bl) + dot(al, bh))


def weight_body(gathered, other, out_high, out_low, inv):
    k = lax.axis_index("row") % 2
    inv[:, k] = gathered[:, 32:48, :]
    inv[:, 1 - k] = other[...]
    inverse = split(inv[...].reshape(512, 512))
    solved = dot3(split(gathered[:, 0:32, :].reshape(512, 512)), inverse, NN)
    high, low = split(dot3(split(solved), inverse, NT))
    out_high[...] = high
    out_low[...] = low


OFFSETS = (0, -4, 4, 8)


def where_am_i():
    row = lax.axis_index("row")
    return row, lax.axis_index("col"), row // 2, row % 2


def place(ref, base, group, core, z, col, high, low, fold):
    for slot in range(4):
        step = OFFSETS[slot]
        far = (0, -1, 1)[group] + step if group < 3 else step - 2 + 4 * core
        at = (z + far + 32) & 15
        hop = 2 * ((at - col) & 15)
        px = (col // 4 + (jnp.int32(TABLE_X) >> hop)) & 3
        py = (col + (jnp.int32(TABLE_Y) >> hop)) & 3
        rows = pl.ds(pl.multiple_of(32 * (4 * px + py), 32), 32)
        start = base + 136 * slot
        for j in range(4):
            tiles = [ref[start + 8 * (4 * i + j):start + 8 * (4 * i + j) + 8, :] for i in range(4)]
            h, l = split(jnp.concatenate(tiles, 0))
            high[rows, 128 * j:128 * j + 128] = h
            low[rows, 128 * j:128 * j + 128] = l
        tile = ref[start + 128:start + 136, :]
        first = pl.multiple_of(16 * (2 * at + core), 16)
        fold[pl.ds(first, 8), :] = tile
        fold[pl.ds(first + 8, 8), :] = pltpu.roll(tile, 64, 1)


def update(half, w, cols, vin, vout, out, sems, row, col):
    lower = 2 * col + half <= row
    copies = []
    for n in range(2):
        part = slice(256 * n, 256 * n + 256)
        span = pl.ds(pl.multiple_of(512 * half + 256 * n, 256), 256)

        @pl.when(lower)
        def _():
            block = tuple(c[part, :] for c in cols)
            vout[:, part] = vin[:, span] - dot3(w, block, NT)

        @pl.when(jnp.logical_not(lower))
        def _():
            vout[:, part] = vin[:, span]

        copy = pltpu.make_async_copy(vout.at[:, part], out.at[:, span], sems.at[n])
        copy.start()
        copies.append(copy)
    return copies


def begin(copies):
    for copy in copies:
        copy.start()


def end(copies):
    for copy in copies:
        copy.wait()


def first_body(wh, wl, vin, mine0, mine1, mine2, mine3, out, fold, high, low, vout, sems):
    row, col, z, k = where_am_i()
    for group, ref in enumerate((mine0, mine1, mine2, mine3)):
        place(ref, 0, group, k, z, col, high, low, fold)
    end(update(k, (wh[...], wl[...]), (high, low), vin, vout, out, sems, row, col))


def second_body(wh, wl, vin, others, half_fold, series, length, part, out, out_s, high, low, vout, fold, vsout, sems):
    row, col, z, k = where_am_i()
    for group in range(4):
        place(others, 544 * group, group, 1 - k, z, col, high, low, fold)
    w = (wh[...], wl[...])
    writes = update(1 - k, w, (high, low), vin, vout, out, sems.at[0:2], row, col)
    for at in range(16):
        rows = pl.ds(pl.multiple_of(32 * at + 16 * k, 16), 16)
        fold[rows, :] = half_fold[rows, :]
    correction = dot3(w, split(fold[...]), NN)
    lengths = jnp.concatenate([length[...], length[...]], 1)
    correction = jnp.where(row < lengths, correction, 0.0)
    vsout[...] = series[...] - correction.T[0:64, :]
    last = pltpu.make_async_copy(vsout, out_s, sems.at[2])
    begin([last])
    end(writes + [last])


def spread_body(panel, stripe, out, stage, sems):
    k = lax.axis_index("row") % 2
    loads = [
        pltpu.make_async_copy(panel, stage.at[0:32, :], sems.at[16]),
        pltpu.make_async_copy(stripe.at[pl.ds(pl.multiple_of(16 * k, 16), 16), :], stage.at[32:48, :], sems.at[17]),
    ]
    begin(loads)
    end(loads)
    copies = [pltpu.make_async_copy(stage, out.at[c], sems.at[c]) for c in range(16)]
    begin(copies)
    end(copies)


VMEM = pl.BlockSpec(memory_space=pltpu.VMEM)
ANY = pl.BlockSpec(memory_space=pl.ANY)


def shape(*dims, dtype=jnp.float32):
    return jax.ShapeDtypeStruct(dims, dtype)


def kernel(body, out, memory, outs, scratch=(), alias=None, room=24):
    specs = {"v": VMEM, "a": ANY}
    out_specs = tuple(specs[m] for m in outs) if len(outs) > 1 else specs[outs]
    limit = room << 20 if room else None

    def call(*args):
        args = [fast(a) if m == "v" else a for a, m in zip(args, memory)]
        return pl.pallas_call(
            body,
            out_shape=out,
            in_specs=[specs[m] for m in memory],
            out_specs=out_specs,
            scratch_shapes=list(scratch),
            input_output_aliases=alias or {},
            compiler_params=pltpu.CompilerParams(vmem_limit_bytes=limit),
        )(*args)

    return call


def block(*dims, dtype=jnp.float32):
    return pltpu.VMEM(dims, dtype)


def sems(n):
    return pltpu.SemaphoreType.DMA((n,))


def tile_order(chunk):
    return chunk.reshape(4, 8, 4, 128).transpose(0, 2, 1, 3).reshape(128, 128)


def step(trailing, panel, inv_factor, later_series, fold_series, fold_len):
    half = jnp.bfloat16
    chunk = tile_order(send(panel, TURN))
    load = kernel(
        spread_body, shape(16, 48, 512), "aa", "a", [block(48, 512), sems(18)], room=0
    )(panel, inv_factor.T)
    gathered = lax.all_to_all(load, "col", 0, 0, tiled=True)
    fold = jnp.concatenate([fold_series[0:8], fold_series[8:16]], 1)
    base = jnp.concatenate([chunk, fold], 0)
    across = send(base, shift(8, 0))
    ahead = send(base, shift(-4))
    behind = send(base, shift(4))
    across = across + send(ahead, shift(-4, 1))
    near = jnp.concatenate([base, behind, ahead, across], 0)
    mine = [near, send(near, shift(1)), send(near, shift(-1)), send(near, PM2)]
    halves = (shape(512, 512, dtype=half), shape(512, 512, dtype=half))
    other = send(gathered[:, 32:, :], SWAP)
    weight = kernel(weight_body, halves, "vv", "vv", [block(16, 2, 16, 512)])(gathered, other)
    held = lax.optimization_barrier(near)
    others = send(jnp.concatenate([held] + mine[1:], 0), SWAP)
    square = block(512, 512, dtype=half)
    work = [square, square, block(512, 512)]
    part, half_fold = kernel(
        first_body, (shape(512, 1024), shape(512, 128)), "vvvvvvv", "av", work + [sems(2)]
    )(*weight, trailing, *mine)
    out, series = kernel(
        second_body,
        (shape(512, 1024), shape(64, 512)),
        "vvvvvvva",
        "aa",
        work + [block(512, 128), block(64, 512), sems(3)],
        {7: 0},
    )(*weight, trailing, others, half_fold, later_series.T, fold_len[None, :], part)
    return out, series.T


def solution(mesh):
    in_specs = (
        P("row", "col"),
        P(("row", "col"), None),
        P(None, "col"),
        P("row", "col"),
        P("row", "col"),
        P("col"),
    )
    out_specs = (P("row", "col"), P("row", "col"))
    return jax.shard_map(step, mesh=mesh, in_specs=in_specs, out_specs=out_specs, check_vma=False)
```
